128 devices in a mesh: side: 2 (over x_lo), seq: 16 (over y, x_hi, core), head: 4 (over z).
Axes of the slice: x: 4 (x_hi: 2, x_lo: 2; x = x_hi * 2 + x_lo), y: 4, z: 4, core: 2. Of those that a mesh axis runs over, the one named last changes fastest.
Arguments:
- cached_hidden: bfloat16 [8, 12288, 8192], P('side', ('seq', 'head')), may hold values from -240 to 240
- page_order: int32 [8, 768], P('side', ('seq', 'head')), may hold values from 0 to 11, as said below
- lengths: int32 [8], P('side'), may hold values from 3072 to 12288, as said below
- new_ids: int32 [8, 4], replicated, may hold values from 0 to 64511
- embedding: bfloat16 [64512, 8192], P('side', ('seq', 'head')), may hold values from -128 to 128
- query_proj: bfloat16 [8192, 8192], P(('seq', 'head')), may hold values from -0.15625 to 0.15625
- down_proj: bfloat16 [8192, 1024], P(('seq', 'head')), may hold values from -0.0625 to 0.0625
- key_up: bfloat16 [8, 64, 128], P('head'), may hold values from -0.75 to 0.75
- value_up: bfloat16 [8, 64, 128], P('head'), may hold values from -1.5 to 1.5
- out_proj: bfloat16 [8192, 8192], P('head', 'seq'), may hold values from -0.0625 to 0.0625
Outputs:
- attended: bfloat16 [8, 4, 8192], P('side', None, 'seq')
The draws below stay inside these ranges and needn't reach their ends.
Inputs may be any that keep to these rules, and one draw needn't show every extreme that they name: `lengths`: each request's number of cached tokens; in every draw some request has exactly 12288. `page_order`: in each row every aligned run of 12 entries holds each number once; entry j of run b names the page of run b's 192 positions in which the request's logical page j of that run is stored.
All inputs are finite; a program needn't handle non-finite values.
Results may differ from the reference program's by a relative error of at most 0.012.
The reference program's roundings to bfloat16 on the way count: a program that leaves them out, or rounds other values in their place, can miss the bound.
Values may be sent and summed in bfloat16 or wider, within the bound.
A program may use at most 128 MiB of HBM per device.

```python
import jax
import jax.numpy as jnp
from jax import lax

D = 8192
HQ = 64
KVH = 8
HD = 128
RANK = 64
VOCAB = 64512
PAGE = 16
NEW = 4
LEN_DEV = 192
REQ = 8
LEN = 12288


def draw_cached_hidden(key, part):
    base_key = jax.random.fold_in(key, 0)
    values = jnp.clip(jax.random.normal(base_key, (REQ, LEN, D), jnp.float32), -6.0, 6.0)
    place = jnp.arange(LEN, dtype=jnp.float32).reshape(1, LEN, 1) / (LEN - 1)
    values = values * 3.0 ** place
    values = jnp.clip(values, -240.0, 240.0)
    return values.astype(jnp.bfloat16)


def draw_page_order(key, part):
    runs = LEN // LEN_DEV
    pages = LEN_DEV // PAGE
    run_keys = jax.random.split(key, REQ * runs)

    def shuffle(one_key):
        return jax.random.permutation(one_key, pages)
    orders = jax.vmap(shuffle)(run_keys)
    return orders.reshape(REQ, runs * pages).astype(jnp.int32)


def draw_lengths(key, part):
    count_key, chosen_key = jax.random.split(jax.random.fold_in(key, 11))
    counts = jax.random.randint(count_key, (REQ,), LEN // 4, LEN + 1)
    chosen = jax.random.randint(chosen_key, (), 0, REQ)
    return jnp.where(jnp.arange(REQ) == chosen, LEN, counts).astype(jnp.int32)


def draw_embedding(key, part):
    base_key, row_key = jax.random.split(key)
    row_scale = 10.0 ** jax.random.uniform(row_key, (VOCAB, 1), jnp.float32)
    column = jnp.arange(D, dtype=jnp.float32) / (D - 1)
    base = jnp.clip(jax.random.normal(base_key, (VOCAB, D), jnp.float32), -5.0, 5.0)
    values = base * row_scale * 3.0 ** column
    values = jnp.clip(values, -128.0, 128.0)
    return values.astype(jnp.bfloat16)


def place_ends(entries, rng, least, largest):
    extent = entries.shape
    spot = [jax.random.randint(jax.random.fold_in(rng, axis), (), 0, extent[axis]) for axis in range(len(extent))]
    entries = entries.at[tuple(spot)].set(least)
    longest = extent.index(max(extent))
    spot[longest] = (spot[longest] + 1) % extent[longest]
    return entries.at[tuple(spot)].set(largest)


def level_of(stream_key, shape, pieces, low, top_value):
    def one(dim, shards_of):
        steps = jax.random.uniform(jax.random.fold_in(jax.random.fold_in(stream_key, 6), dim), (shards_of,), jnp.float32, low / len(pieces), top_value / len(pieces))
        return jnp.repeat(jnp.exp(steps), shape[dim] // shards_of).reshape((-1,) + (1,) * (len(shape) - dim - 1))

    level = one(*pieces[0])
    for cut in pieces[1:]:
        level = level * one(*cut)
    return level


def centred(rng, shape, width, limit, pieces=(), held_as=jnp.bfloat16):
    factor_of = level_of(rng, shape, pieces, -0.22, 0.18) if pieces else 1.0
    drawn = jax.random.normal(rng, shape, jnp.float32) * width * factor_of
    return jnp.minimum(jnp.maximum(drawn, -limit), limit).astype(held_as)


def setup_inputs(seed: int = 0) -> dict:
    key_list = jax.random.split(jax.random.key(seed), 11)
    return {
        "cached_hidden": draw_cached_hidden(jax.random.fold_in(key_list[10], 71), 0),
        "page_order": draw_page_order(jax.random.fold_in(key_list[10], 71), 0),
        "lengths": draw_lengths(jax.random.fold_in(key_list[10], 71), 0),
        "new_ids": place_ends(jax.random.randint(key_list[3], (REQ, NEW), 0, VOCAB), jax.random.fold_in(key_list[3], 1), 0, VOCAB - 1).astype(jnp.int32),
        "embedding": draw_embedding(jax.random.fold_in(key_list[10], 71), 0),
        "query_proj": centred(key_list[5], (D, HQ * HD), (D // 6) ** -0.5, 0.15625, ((0, 64),)),
        "down_proj": centred(key_list[6], (D, KVH * 2 * RANK), D ** -0.5, 0.0625, ((0, 64),)),
        "key_up": centred(key_list[7], (KVH, RANK, HD), RANK ** -0.5, 0.75, ((0, 4),)),
        "value_up": centred(key_list[8], (KVH, RANK, HD), (RANK // 4) ** -0.5, 1.5, ((0, 4),)),
        "out_proj": centred(key_list[9], (HQ * HD, D), (HQ * HD) ** -0.5, 0.0625, ((0, 4), (1, 16))),
    }


rope_base = 500000.0
masked_score = -1e+30

def rotate(values, positions):
    half_width = values.shape[-1] // 2
    frequency = 1.0 / rope_base ** (jnp.arange(half_width, dtype=jnp.float32) * 2.0 / values.shape[-1])
    angles = positions.astype(jnp.float32)[..., None] * frequency
    cosine = jnp.cos(angles)
    sines = jnp.sin(angles)
    lower_half = values[..., :half_width]
    upper_half = values[..., half_width:]
    return jnp.concatenate([lower_half * cosine - upper_half * sines, upper_half * cosine + lower_half * sines], axis=-1)

def settle(values):
    return lax.optimization_barrier(values.astype(jnp.bfloat16))

def rebuild(latent, positions, key_up, value_up):
    key_part = latent[..., :RANK].astype(jnp.float32)
    value_part = latent[..., RANK:].astype(jnp.float32)
    rebuilt_keys = jnp.einsum('pgc,gcd->pgd', key_part, key_up.astype(jnp.float32))
    rebuilt_keys = settle(rotate(rebuilt_keys, positions[:, None]))
    rebuilt_values = settle(jnp.einsum('pgc,gcd->pgd', value_part, value_up.astype(jnp.float32)))
    return (rebuilt_keys, rebuilt_values)

def reference(cached_hidden, page_order, lengths, new_ids, embedding, query_proj, down_proj, key_up, value_up, out_proj):
    group_heads = HQ // KVH
    embedded = jnp.take(embedding, new_ids.reshape(-1), axis=0)
    widened = embedded.astype(jnp.float32)
    inv_rms = lax.rsqrt(lax.optimization_barrier(jnp.mean(widened * widened, axis=-1)) + 1e-05).reshape(REQ, NEW)
    query_raw = jnp.dot(embedded, query_proj, preferred_element_type=jnp.float32).reshape(REQ, NEW, HQ, HD)
    fresh_positions = lengths[:, None] + jnp.arange(NEW, dtype=jnp.int32)[None, :]
    queries = settle(rotate(query_raw * inv_rms[:, :, None, None], fresh_positions[..., None]))
    fresh_raw = jnp.dot(embedded, down_proj, preferred_element_type=jnp.float32).reshape(REQ, NEW, KVH, 2 * RANK)
    fresh_latent = settle(fresh_raw * inv_rms[:, :, None, None])

    def project(hidden_rows):
        return jnp.dot(hidden_rows, down_proj, preferred_element_type=jnp.float32).astype(jnp.bfloat16)
    cached_latent = lax.map(project, cached_hidden)
    position_ids = jnp.arange(LEN, dtype=jnp.int32)
    scaling = 1.0 / HD ** 0.5
    causal = jnp.arange(NEW, dtype=jnp.int32)[:, None] >= jnp.arange(NEW, dtype=jnp.int32)[None, :]

    def attend(request_item):
        latent_rows, order_row, length, query_rows, fresh_rows, fresh_pos = request_item
        physical = position_ids // LEN_DEV * LEN_DEV + jnp.take(order_row, position_ids // PAGE) * PAGE + position_ids % PAGE
        ordered = jnp.take(latent_rows, physical.astype(jnp.int32), axis=0).reshape(LEN, KVH, 2 * RANK)
        cache_keys, cache_values = rebuild(ordered, position_ids, key_up, value_up)
        fresh_keys, fresh_values = rebuild(fresh_rows, fresh_pos, key_up, value_up)
        grouped = query_rows.reshape(NEW, KVH, group_heads, HD).astype(jnp.float32)
        cache_scores = jnp.einsum('tgjd,pgd->tgjp', grouped, cache_keys.astype(jnp.float32)) * scaling
        fresh_scores = jnp.einsum('tgjd,ugd->tgju', grouped, fresh_keys.astype(jnp.float32)) * scaling
        live = (position_ids < length)[None, None, None, :]
        seen = causal[:, None, None, :]
        cache_scores = jnp.where(live, cache_scores, masked_score)
        fresh_scores = jnp.where(seen, fresh_scores, masked_score)
        row_peak = jnp.maximum(lax.optimization_barrier(jnp.max(cache_scores, axis=-1)), lax.optimization_barrier(jnp.max(fresh_scores, axis=-1)))
        cache_weights = jnp.where(live, jnp.exp(cache_scores - row_peak[..., None]), 0.0)
        fresh_weights = jnp.where(seen, jnp.exp(fresh_scores - row_peak[..., None]), 0.0)
        totals = lax.optimization_barrier(jnp.sum(cache_weights, axis=-1)) + lax.optimization_barrier(jnp.sum(fresh_weights, axis=-1))
        summed = jnp.einsum('tgjp,pgd->tgjd', settle(cache_weights).astype(jnp.float32), cache_values.astype(jnp.float32))
        summed = summed + jnp.einsum('tgju,ugd->tgjd', settle(fresh_weights).astype(jnp.float32), fresh_values.astype(jnp.float32))
        return settle(summed / totals[..., None]).reshape(NEW, HQ * HD)
    context = lax.map(attend, (cached_latent, page_order, lengths, queries, fresh_latent, fresh_positions))
    attended = jnp.dot(context.reshape(REQ * NEW, HQ * HD), out_proj, preferred_element_type=jnp.float32)
    return attended.astype(jnp.bfloat16).reshape(REQ, NEW, D)
```

```python
import functools
import math

import jax
import jax.numpy as jnp
from jax import lax
from jax.experimental import pallas as pl
from jax.experimental.pallas import tpu as pltpu
from jax.sharding import Mesh
from jax.sharding import PartitionSpec as P

D = 8192
HD = 128
PAGE = 16
SEQ = ("seq_0", "seq_1", "seq_2")
SIDE_SEQ_HEAD = ("side", "seq_0", "seq_1", "seq_2", "head")
SEQ_HEAD = ("seq_0", "seq_1", "seq_2", "head")
AXES = ("side", "seq_0", "seq_1", "seq_2", "head")
MESH = pl.DeviceIdType.MESH
rope_base = 500000.0
masked_score = -1e30
BF = jnp.bfloat16
F32 = jnp.float32


def pick_kernel(ids_ref, emb_ref, out_ref, blocks, rows, sems):
    vocab = emb_ref.shape[0]
    first = lax.axis_index("side") * vocab
    count = blocks.shape[0]
    width = ids_ref.shape[1]
    subs = []
    copies = []
    for i in range(count):
        raw = ids_ref[i // width, i % width] - first
        inside = jnp.logical_and(raw >= 0, raw < vocab)
        local = jnp.clip(raw, 0, vocab - 1)
        block = local // 16
        subs.append(jnp.where(inside, local - block * 16, -1))
        copy = pltpu.make_async_copy(
            emb_ref.at[pl.ds(pl.multiple_of(block * 16, 16), 16)], blocks.at[i], sems.at[i]
        )
        copy.start()
        copies.append(copy)
    line = lax.broadcasted_iota(jnp.int32, (16, HD), 0)
    for i in range(count):
        copies[i].wait()
        part = jnp.where(line == subs[i], blocks[i].astype(F32), 0.0)
        rows[pl.ds(i, 1), :] = jnp.sum(part, axis=0, keepdims=True)
    out_ref[...] = rows[...].astype(BF)


def pick(new_ids, embedding):
    count = new_ids.size
    return pl.pallas_call(
        pick_kernel,
        out_shape=jax.ShapeDtypeStruct((count, HD), BF),
        in_specs=[
            pl.BlockSpec(memory_space=pltpu.SMEM),
            pl.BlockSpec(memory_space=pl.ANY),
        ],
        out_specs=pl.BlockSpec(memory_space=pltpu.VMEM),
        scratch_shapes=[
            pltpu.VMEM((count, 16, HD), BF),
            pltpu.VMEM((count, HD), F32),
            pltpu.SemaphoreType.DMA((count,)),
        ],
        name="pick_rows",
    )(new_ids, embedding)


def rope(values, cosine, sine):
    return values * cosine + pltpu.roll(values, HD // 2, 1) * sine


def split_scalar(column):
    lane = lax.broadcasted_iota(jnp.int32, (column.shape[0], HD), 1)
    wide = jnp.broadcast_to(column, lane.shape)
    high = wide.astype(BF).astype(F32)
    middle = (wide - high).astype(BF).astype(F32)
    low = wide - high - middle
    return jnp.where(lane == 0, high, jnp.where(lane == 1, middle, low)).astype(BF)


def joined_scalar(block):
    part = block[:, HD:].astype(F32)
    return part[:, 0:1] + part[:, 1:2] + part[:, 2:3]


def merged(blocks):
    levels = [joined_scalar(b) for b in blocks]
    peak = functools.reduce(jnp.maximum, levels)
    weights = [jnp.exp(level - peak) for level in levels]
    total = functools.reduce(jnp.add, weights)
    summed = functools.reduce(
        jnp.add, [w * b[:, :HD].astype(F32) for w, b in zip(weights, blocks)]
    )
    return summed / total, peak + jnp.log(total)


STEPS = (
    (0, 0), (1, 0), (0, 1), (2, 0), (0, 2), (3, 0), (1, 1), (1, 2),
    (0, 3), (1, 3), (2, 1), (2, 2), (2, 3), (3, 1), (3, 2), (3, 3),
)
PART1 = (0, 4, 8, 12)
PART2 = (2, 6, 10, 13)


def pick_int(n, values):
    found = jnp.int32(values[0])
    for j in range(1, len(values)):
        found = jnp.where(n == j, jnp.int32(values[j]), found)
    return found


def offset_of(k):
    return k // 2 + 3 * (k % 2) - 2 * (k // 3)


def main_kernel(
    hid, down, picked, qproj, kv, outp, tab, bias_a, bias_b, ftab,
    out_ref,
    H, W, acc, QP, OP, kvb, ptab, pbias, pickb, part, rcore, qsum, rz, ry, rx, qz,
    Bm, FK, FV, Q, ob, cz, cmine, cy, cmine2, cx, ctx, fin,
    lsem, wl, hs, hr, ws, wr, xs, ps, pr, fs, fr, es, er,
):
    s, y, x, c, z = [lax.axis_index(a) for a in AXES]
    o = 1 - c

    def dev(s_=s, y_=y, x_=x, c_=c, z_=z):
        return (s_, y_, x_, c_, z_)

    core_dev = dev(c_=o)
    pair_dev = dev(s_=1 - s)
    cross_dev = dev(s_=1 - s, x_=1 - x)
    xhi_dev = dev(x_=1 - x)
    z_dev = [dev(z_=lax.rem(z + d, 4)) for d in (1, 2, 3)]
    y_dev = [dev(y_=lax.rem(y + d, 4)) for d in (1, 2, 3)]

    def remote(src, dst, send, recv, device):
        return pltpu.make_async_remote_copy(
            src_ref=src, dst_ref=dst, send_sem=send, recv_sem=recv,
            device_id=device, device_id_type=MESH,
        )

    qcopy = pltpu.make_async_copy(qproj, QP, lsem.at[4])
    qcopy.start()

    def ychunk(q):
        yy = lax.rem(y + (0, 3, 1, 2)[q], 4)
        return pl.ds(pl.multiple_of(yy * 2048, 2048), 2048)

    hlocal = [
        pltpu.make_async_copy(hid.at[:, ychunk(q)], H.at[0, :, ychunk(q)], lsem.at[q])
        for q in range(4)
    ]
    for copy in hlocal:
        copy.start()
    ocopy = pltpu.make_async_copy(outp, OP, lsem.at[5])
    ocopy.start()

    everyone = [core_dev, pair_dev, cross_dev, xhi_dev] + z_dev + y_dev
    barrier = pltpu.get_barrier_semaphore()
    for device in everyone:
        pl.semaphore_signal(barrier, inc=1, device_id=device, device_id_type=MESH)
    pl.semaphore_wait(barrier, len(everyone))

    sent = []

    def go(copy):
        copy.start()
        sent.append(copy)
        return copy

    ex = [0]

    def message(src, dst, device):
        k = ex[0]
        ex[0] += 1
        return remote(src, dst, es.at[k], er.at[k], device)

    m_pick = go(message(picked, pickb, pair_dev))
    own_rows = pl.ds(pl.multiple_of(c * 128, 128), 128)
    w_local = []
    w_init = []
    for i in range(4):
        theirs = pl.ds(pl.multiple_of((2 * i + o) * 128, 128), 128)
        w_init.append(go(remote(
            down.at[:, theirs], W.at[x, y, z, own_rows, pl.ds(i * 128, 128)],
            ws.at[i], wr.at[i], core_dev,
        )))
    for i in range(4):
        mine = pl.ds(pl.multiple_of((2 * i + c) * 128, 128), 128)
        copy = pltpu.make_async_copy(
            down.at[:, mine], W.at[x, y, z, own_rows, pl.ds(i * 128, 128)], wl.at[i]
        )
        copy.start()
        w_local.append(copy)
    hremote = [
        remote(hid.at[:, ychunk(q)], H.at[1, :, ychunk(q)], hs.at[q], hr.at[q], core_dev)
        for q in range(4)
    ]
    go(hremote[0])
    m_kv = [go(message(kv.at[c], kvb.at[z], z_dev[d])) for d in range(3)]

    in_plane = pl.ds(pl.multiple_of(s * 64, 64), 192)
    prow = pl.ds(pl.multiple_of(s * 224, 32), 32)
    crow = pl.ds(pl.multiple_of(32 + s * 160, 32), 32)
    ia = z * o + y * c
    ib = y * o + z * c

    def place(a_off, b_off):
        a_at = lax.rem(ia + a_off, 4)
        b_at = lax.rem(ib + b_off, 4)
        return (b_at * o + a_at * c, a_at * o + b_at * c)

    def unit(u):
        return x + u - 2 * x * u

    def a_dev(step):
        return dev(y_=lax.rem(y + step * c, 4), z_=lax.rem(z + step * o, 4))

    def b_dev(step):
        return dev(y_=lax.rem(y + step * o, 4), z_=lax.rem(z + step * c, 4))

    def piece(line, m, along_a, a_off):
        u = (0, 1, 0, 1, 0, 1)[m]
        step = (1, 1, 3, 3, 1, 3)[m]
        off = (0, 0, 0, 0, 3, 1)[m]
        if along_a:
            at = place(off, 0)
            device = a_dev(step)
        else:
            at = place(a_off, off)
            device = b_dev(step)
        ref = W.at[unit(u), at[0], at[1], in_plane]
        return remote(ref, ref, ps.at[line, m], pr.at[line, m], device)

    def a_piece(m):
        return piece(4, m, True, None)

    def b_piece(k, m):
        return piece(k, m, False, offset_of(k))

    def side_piece(k, b, which):
        at = place(offset_of(k), offset_of(b))
        rows = prow if which == 0 else crow
        ref = W.at[:, at[0], at[1], rows]
        return remote(
            ref, ref, fs.at[k, b, which], fr.at[k, b, which], pair_dev if which == 0 else cross_dev
        )

    def side_start(k, b):
        side_piece(k, b, 0).start()
        side_piece(k, b, 1).start()

    for copy in w_local:
        copy.wait()
    for copy in w_init:
        copy.wait_recv()
    own = W.at[x, y, z]
    m_cross = go(remote(own, own, xs.at[0], xs.at[1], cross_dev))
    for m in (0, 2):
        a_piece(m).start()
        b_piece(0, m).start()

    m_pick.wait_recv()
    both = (picked[...].astype(F32) + pickb[...].astype(F32)).astype(BF)
    pickb[...] = both
    rows16 = pickb[pl.ds(pl.multiple_of(s * 16, 16), 16), :]
    wide16 = rows16.astype(F32)
    squares = wide16 * wide16
    qcopy.wait()
    for cc in (0, 1):
        for i in range(4):
            g = 2 * i + cc
            part[cc, i, :, 0:1024] = jnp.dot(
                rows16, QP[:, g * 1024 : (g + 1) * 1024], preferred_element_type=F32
            )
            part[cc, i, :, 1024:1152] = jnp.dot(
                rows16, down[:, g * 128 : (g + 1) * 128], preferred_element_type=F32
            )
            part[cc, i, :, 1152:1280] = squares
    m_core = go(message(part.at[o], rcore, core_dev))
    m_tab = go(message(tab, ptab, core_dev))
    m_bias = go(message(bias_b, pbias, core_dev))
    for q in (1, 2, 3):
        go(hremote[q])

    m_cross.wait_recv()
    for m in (1, 3):
        a_piece(m).start()
        b_piece(0, m).start()

    a_piece(0).wait_recv()
    a_piece(4).start()
    b_piece(1, 0).start()
    b_piece(1, 2).start()
    a_piece(2).wait_recv()
    b_piece(2, 0).start()
    b_piece(2, 2).start()

    m_core.wait_recv()
    for i in range(4):
        qsum[i] = part[c, i] + rcore[i]
    m_z = [
        go(message(qsum.at[lax.rem(z + d, 4)], rz.at[d - 1], z_dev[d - 1])) for d in (1, 2, 3)
    ]

    a_piece(1).wait_recv()
    b_piece(1, 1).start()
    b_piece(1, 3).start()
    side_start(1, 0)
    a_piece(3).wait_recv()
    a_piece(5).start()
    b_piece(2, 1).start()
    b_piece(2, 3).start()
    side_start(2, 0)

    for m in m_z:
        m.wait_recv()
    rz[3] = qsum[z] + rz[0] + rz[1] + rz[2]
    m_y = [go(message(rz.at[3], ry.at[d - 1], y_dev[d - 1])) for d in (1, 2, 3)]

    a_piece(4).wait_recv()
    b_piece(3, 0).start()
    b_piece(3, 2).start()
    a_piece(5).wait_recv()
    b_piece(3, 1).start()
    b_piece(3, 3).start()
    side_start(3, 0)

    for m in m_y:
        m.wait_recv()
    ry[3] = rz[3] + ry[0] + ry[1] + ry[2]
    m_x = go(message(ry.at[3], rx, xhi_dev))

    lines = [st[0] for st in STEPS]
    places = [st[1] for st in STEPS]

    m_q = [message(qz.at[z], qz.at[z], z_dev[d - 1]) for d in (1, 2, 3)]
    sent.extend(m_q)

    def step(n, carry):
        for k in range(4):
            @pl.when(n == PART1[k])
            def _():
                b_piece(k, 0).wait_recv()
                b_piece(k, 4).start()
                b_piece(k, 3).wait_recv()
                b_piece(k, 5).start()
                b_piece(k, 1).wait_recv()
                side_start(k, 1)
                b_piece(k, 2).wait_recv()
                side_start(k, 2)

            @pl.when(n == PART2[k])
            def _():
                b_piece(k, 4).wait_recv()
                b_piece(k, 5).wait_recv()
                side_start(k, 3)

        @pl.when(n == 1)
        def _():
            m_x.wait_recv()
            total = ry[3] + rx[...]
            inverse = lax.rsqrt(
                jnp.sum(total[:, 1152:1280], axis=1, keepdims=True) / D + 1e-05
            )
            cosine = ftab[:, 0:128]
            sine = ftab[:, 128:256]
            for j in range(8):
                head = total[:, j * 128 : (j + 1) * 128] * inverse
                qz[z, :, j * 128 : (j + 1) * 128] = rope(head, cosine, sine).astype(BF)
            qz[z, :, 1024:1152] = (total[:, 1024:1152] * inverse).astype(BF)
            for m in m_q:
                m.start()

        for q, at in enumerate((0, 1, 3, 5)):
            @pl.when(n == at)
            def _():
                hlocal[q].wait()
                hremote[q].wait_recv()

        k = pick_int(n, lines)
        b = pick_int(n, places)

        @pl.when(n > 0)
        def _():
            side_piece(k, b, 0).wait_recv()
            side_piece(k, b, 1).wait_recv()

        yy, zz = place(offset_of(k), offset_of(b))

        def columns(xh, core):
            return pl.ds(pl.multiple_of((((yy * 2 + xh) * 2 + core) * 4 + zz) * 128, 128), 128)

        def tile(m, carry):
            t = m // 2
            rows = pl.ds(pl.multiple_of((m % 2) * 384, 384), 384)
            left = [
                jnp.concatenate([H[t, rows, columns(xh, 0)], H[t, rows, columns(xh, 1)]], axis=1)
                for xh in (0, 1)
            ]
            product = jnp.dot(left[0], W[0, yy, zz], preferred_element_type=F32) + jnp.dot(
                left[1], W[1, yy, zz], preferred_element_type=F32
            )

            @pl.when(n == 0)
            def _():
                acc[t, rows, :] = product

            @pl.when(n > 0)
            def _():
                acc[t, rows, :] += product

            return carry

        lax.fori_loop(0, 4, tile, 0)
        return carry

    lax.fori_loop(0, 16, step, 0)

    for m in m_kv:
        m.wait_recv()
    kvb[z] = kv[c]
    for m in m_q:
        m.wait_recv()
    m_tab.wait_recv()
    m_bias.wait_recv()
    pbias[...] = pbias[...] + bias_a[...]
    line = lax.broadcasted_iota(jnp.int32, (128, 128), 0)
    lane = lax.broadcasted_iota(jnp.int32, (128, 128), 1)
    to_requests = (
        lane == (line % 32) // 4 * 16 + line // 32 * 4 + line % 4
    ).astype(F32).astype(BF)
    to_heads = (
        lane == (line % 16) // 4 * 32 + line // 16 * 4 + line % 4
    ).astype(F32).astype(BF)
    for i in range(4):
        weights = kvb[i]
        zero = jnp.zeros_like(weights)
        Bm[i, :, 0:128] = jnp.where(line < 64, weights, zero)
        Bm[i, :, 128:256] = jnp.where(line < 64, zero, weights)
        heads = jnp.concatenate([qz[i, :, j * 128 : (j + 1) * 128] for j in range(8)], axis=0)
        Q[i] = jnp.dot(to_requests, heads, preferred_element_type=F32).astype(BF)
        fresh = jnp.dot(qz[i, :, 1024:1152], Bm[i], preferred_element_type=F32)
        pad = jnp.zeros((112, 128), BF)
        FK[i] = jnp.concatenate(
            [rope(fresh[:, 0:128], ftab[:, 0:128], ftab[:, 128:256]).astype(BF), pad], axis=0
        )
        FV[i] = jnp.concatenate([fresh[:, 128:256].astype(BF), pad], axis=0)

    elsewhere = jnp.where((y + x + z) == 0, 0.0, masked_score)
    row32 = lax.broadcasted_iota(jnp.int32, (32, 128), 0)
    col32 = lax.broadcasted_iota(jnp.int32, (32, 128), 1)
    scaling = 1.0 / math.sqrt(HD)

    def request(r, carry):
        rows = pl.ds(pl.multiple_of(r * 192, 64), 192)
        cosine = jnp.concatenate([tab[rows, 0:128], ptab[rows, 0:128]], axis=0)
        sine = jnp.concatenate([tab[rows, 128:256], ptab[rows, 128:256]], axis=0)
        seen = (col32 // 4 == r) & (col32 % 4 <= row32 % 4)
        mask = jnp.concatenate(
            [
                jnp.broadcast_to(pbias[pl.ds(r, 1), :], (32, 384)),
                jnp.where(seen, elsewhere, masked_score),
            ],
            axis=1,
        )
        for i in range(4):
            latent = jnp.concatenate(
                [acc[0, rows, i * 128 : (i + 1) * 128], acc[1, rows, i * 128 : (i + 1) * 128]],
                axis=0,
            ).astype(BF)
            rebuilt = jnp.dot(latent, Bm[i], preferred_element_type=F32)
            keys = jnp.concatenate(
                [rope(rebuilt[:, 0:128], cosine, sine).astype(BF), FK[i]], axis=0
            )
            values = jnp.concatenate([rebuilt[:, 128:256].astype(BF), FV[i]], axis=0)
            query = Q[i, pl.ds(pl.multiple_of(r * 32, 32), 32), :]
            scores = lax.dot_general(
                query, keys, (((1,), (1,)), ((), ())), preferred_element_type=F32
            ) * scaling + mask
            peak = jnp.max(scores, axis=1, keepdims=True)
            e = jnp.where(mask > -1e29, jnp.exp(scores - peak), 0.0)
            total = jnp.sum(e, axis=1, keepdims=True)
            context = jnp.dot(e.astype(BF), values, preferred_element_type=F32)
            some = total > 0.0
            safe = jnp.where(some, total, 1.0)
            level = jnp.where(some, peak + jnp.log(safe), masked_score)
            at = pl.ds(pl.multiple_of(r * 32, 32), 32)
            ob[i, at, 0:128] = (context / safe).astype(BF)
            ob[i, at, 128:256] = split_scalar(level)
        return carry

    lax.fori_loop(0, 4, request, 0)

    m_cz = [
        go(message(ob.at[lax.rem(z + d, 4)], cz.at[d - 1], z_dev[d - 1])) for d in (1, 2, 3)
    ]
    for m in m_cz:
        m.wait_recv()
    value, level = merged([ob[z], cz[0], cz[1], cz[2]])
    cmine[:, 0:128] = value.astype(BF)
    cmine[:, 128:256] = split_scalar(level)
    m_cy = [go(message(cmine, cy.at[d - 1], y_dev[d - 1])) for d in (1, 2, 3)]
    for m in m_cy:
        m.wait_recv()
    value, level = merged([cmine[...], cy[0], cy[1], cy[2]])
    cmine2[:, 0:128] = value.astype(BF)
    cmine2[:, 128:256] = split_scalar(level)
    m_cx = go(message(cmine2, cx, xhi_dev))
    m_cx.wait_recv()
    value, _ = merged([cmine2[...], cx[...]])
    ctx[c] = jnp.dot(to_heads, value.astype(BF), preferred_element_type=F32).astype(BF)
    m_ctx = go(message(ctx.at[c], ctx.at[c], core_dev))
    m_ctx.wait_recv()
    ocopy.wait()
    left = jnp.concatenate(
        [ctx[g, j * 16 : (j + 1) * 16, :] for g in range(2) for j in range(8)], axis=1
    )
    fin[z] = jnp.dot(left, OP[...], preferred_element_type=F32)
    m_fin = [go(message(fin.at[z], fin.at[z], z_dev[d - 1])) for d in (1, 2, 3)]
    for m in m_fin:
        m.wait_recv()
    out_ref[...] = (fin[0] + fin[1] + fin[2] + fin[3]).astype(BF)

    for copy in sent:
        copy.wait_send()
    for m in range(6):
        a_piece(m).wait_send()

    def drain(k, carry):
        for m in range(6):
            b_piece(k, m).wait_send()
        for b in range(4):
            @pl.when(k + b > 0)
            def _():
                side_piece(k, b, 0).wait_send()
                side_piece(k, b, 1).wait_send()
        return carry

    lax.fori_loop(0, 4, drain, 0)


MESSAGES = 1 + 3 + 3 + 3 + 3 + 1 + 3 + 3 + 3 + 1 + 1 + 3


def main(hid, down, picked, qproj, kv, outp, tab, bias_a, bias_b, ftab):
    vm = pl.BlockSpec(memory_space=pltpu.VMEM)
    anyspace = pl.BlockSpec(memory_space=pl.ANY)
    V = pltpu.VMEM
    S = pltpu.SemaphoreType.DMA
    return pl.pallas_call(
        main_kernel,
        out_shape=jax.ShapeDtypeStruct((16, 512), BF),
        in_specs=[anyspace, vm, vm, anyspace, vm, anyspace, vm, vm, vm, vm],
        out_specs=vm,
        scratch_shapes=[
            V((2, 768, 8192), BF),
            V((2, 4, 4, 256, 512), BF),
            V((2, 768, 512), F32),
            V((128, 8192), BF),
            V((2048, 512), BF),
            V((4, 128, 128), BF),
            V((768, 256), F32),
            V((8, 384), F32),
            V((32, 128), BF),
            V((2, 4, 16, 1280), F32),
            V((4, 16, 1280), F32),
            V((4, 16, 1280), F32),
            V((4, 16, 1280), F32),
            V((4, 16, 1280), F32),
            V((16, 1280), F32),
            V((4, 16, 1152), BF),
            V((4, 128, 256), BF),
            V((4, 128, 128), BF),
            V((4, 128, 128), BF),
            V((4, 128, 128), BF),
            V((4, 128, 256), BF),
            V((3, 128, 256), BF),
            V((128, 256), BF),
            V((3, 128, 256), BF),
            V((128, 256), BF),
            V((128, 256), BF),
            V((2, 128, 128), BF),
            V((4, 16, 512), F32),
            S((6,)),
            S((4,)),
            S((4,)),
            S((4,)),
            S((4,)),
            S((4,)),
            S((2,)),
            S((5, 6)),
            S((5, 6)),
            S((4, 4, 2)),
            S((4, 4, 2)),
            S((MESSAGES,)),
            S((MESSAGES,)),
        ],
        compiler_params=pltpu.CompilerParams(
            collective_id=0, has_side_effects=True, vmem_limit_bytes=62 * 2**20
        ),
        name="gather_decode",
    )(hid, down, picked, qproj, kv, outp, tab, bias_a, bias_b, ftab)


def rope_table(positions):
    half = HD // 2
    frequency = 1.0 / rope_base ** (jnp.arange(half, dtype=F32) * 2.0 / HD)
    angles = positions.astype(F32)[:, None] * frequency
    cosine = jnp.cos(angles)
    sine = jnp.sin(angles)
    return jnp.concatenate([cosine, cosine, -sine, sine], axis=1)


def local(
    cached_hidden, page_order, lengths, new_ids, embedding,
    query_proj, down_proj, key_up, value_up, out_proj,
):
    requests, span, width = cached_hidden.shape
    steps = new_ids.shape[1]
    pages = span // PAGE
    picked = pick(new_ids, embedding)
    run = lax.axis_index(SEQ_HEAD)
    slots = jnp.arange(pages, dtype=jnp.int32)
    logical = jnp.sum(
        jnp.where(page_order[:, None, :] == slots[None, :, None], slots[None, None, :], 0), axis=2
    )
    positions = (
        run * span + logical[:, :, None] * PAGE + jnp.arange(PAGE, dtype=jnp.int32)[None, None, :]
    ).reshape(requests, span)
    tab = rope_table(positions.reshape(-1))
    bias = jnp.where(positions < lengths[:, None], 0.0, masked_score).astype(F32)
    bias_a = jnp.pad(bias, ((0, 4), (0, span)))
    bias_b = jnp.pad(bias, ((0, 4), (span, 0)))
    fresh = (lengths[:, None] + jnp.arange(steps, dtype=jnp.int32)[None, :]).reshape(-1)
    ftab = rope_table(fresh)
    kv = jnp.concatenate([key_up, value_up], axis=1)
    out = main(
        cached_hidden.reshape(requests * span, width), down_proj, picked, query_proj, kv,
        out_proj, tab, bias_a, bias_b, ftab,
    )
    return out.reshape(requests, steps, -1)


def solution(mesh):
    finer = Mesh(
        mesh.devices.reshape(mesh.shape["side"], 4, 2, 2, mesh.shape["head"]), AXES
    )
    placed = (
        P("side", SEQ_HEAD, None),
        P("side", SEQ_HEAD),
        P("side"),
        P(),
        P("side", SEQ_HEAD),
        P(SEQ_HEAD, None),
        P(SEQ_HEAD, None),
        P("head", None, None),
        P("head", None, None),
        P("head", SEQ),
    )
    return jax.shard_map(
        local, mesh=finer, in_specs=placed, out_specs=P("side", None, SEQ), check_vma=False
    )
```

```python
import functools
import math

import jax
import jax.numpy as jnp
import numpy as np
from jax import lax
from jax.experimental import pallas as pl
from jax.experimental.pallas import tpu as pltpu
from jax.sharding import Mesh
from jax.sharding import PartitionSpec as P

D = 8192
HD = 128
PAGE = 16
SEQ = ("seq_0", "seq_1", "seq_2")
SIDE_SEQ_HEAD = ("side", "seq_0", "seq_1", "seq_2", "head")
SEQ_HEAD = ("seq_0", "seq_1", "seq_2", "head")
AXES = ("side", "seq_0", "seq_1", "seq_2", "head")
MESH = pl.DeviceIdType.MESH
rope_base = 500000.0
masked_score = -1e30
BF = jnp.bfloat16
F32 = jnp.float32


def prepare_kernel(
    ids_ref, order_ref, lengths_ref, freq_ref, emb_ref,
    out_ref, page_ref, fresh_ref, bias_ref,
    blocks, rows, line_at, sems,
):
    vocab = emb_ref.shape[0]
    first = lax.axis_index("side") * vocab
    count = blocks.shape[0]
    steps = ids_ref.shape[0]
    requests, pages = order_ref.shape
    span = pages * PAGE
    start = lax.axis_index(SEQ_HEAD) * span
    subs = []
    copies = []
    for i in range(count):
        raw = ids_ref[i % steps, i // steps] - first
        inside = jnp.logical_and(raw >= 0, raw < vocab)
        local = jnp.clip(raw, 0, vocab - 1)
        block = local // 16
        subs.append(jnp.where(inside, local - block * 16, -1))
        copy = pltpu.make_async_copy(
            emb_ref.at[pl.ds(pl.multiple_of(block * 16, 16), 16)], blocks.at[i], sems.at[i]
        )
        copy.start()
        copies.append(copy)
    lane = lax.broadcasted_iota(jnp.int32, (1, 384), 1)
    bias_ref[...] = jnp.zeros_like(bias_ref)
    for r in range(requests):
        at = jnp.zeros((1, 384), jnp.int32)
        for j in range(pages):
            k = order_ref[r, j]
            line_at[pl.ds(r * pages + k, 1), :] = jnp.full((1, HD), start + j * PAGE, jnp.int32)
            at = jnp.where(
                (lane // PAGE) % pages == k, start + j * PAGE + lane % PAGE, at
            )
        dead = jnp.where(at < lengths_ref[r], 0.0, masked_score)
        bias_ref[0, pl.ds(r, 1), :] = jnp.where(lane < span, dead, 0.0)
        bias_ref[1, pl.ds(r, 1), :] = jnp.where(lane >= span, dead, 0.0)
        for t in range(steps):
            line_at[pl.ds(requests * pages + r * steps + t, 1), :] = jnp.full(
                (1, HD), lengths_ref[r] + t, jnp.int32
            )
    offset = lax.broadcasted_iota(jnp.int32, (PAGE, HD), 0)
    line_at[pl.ds(64, PAGE), :] = offset
    angles = line_at[...].astype(F32) * freq_ref[0:1, :]
    cosine = jnp.cos(angles)
    sine = jnp.sin(angles)
    page_ref[:, 0:HD] = cosine
    page_ref[:, HD : 2 * HD] = sine
    half = lax.broadcasted_iota(jnp.int32, (16, HD), 1) < HD // 2
    fresh_ref[:, 0:HD] = cosine[48:64]
    fresh_ref[:, HD : 2 * HD] = jnp.where(half, -sine[48:64], sine[48:64])
    line = lax.broadcasted_iota(jnp.int32, (16, HD), 0)
    for i in range(count):
        copies[i].wait()
        part = jnp.where(line == subs[i], blocks[i].astype(F32), 0.0)
        rows[pl.ds(i, 1), :] = jnp.sum(part, axis=0, keepdims=True)
    out_ref[...] = rows[...].astype(BF)


def prepare(new_ids, page_order, lengths, freq, embedding):
    count = new_ids.size
    smem = pl.BlockSpec(memory_space=pltpu.SMEM)
    vm = pl.BlockSpec(memory_space=pltpu.VMEM)
    return pl.pallas_call(
        prepare_kernel,
        out_shape=(
            jax.ShapeDtypeStruct((count, HD), BF),
            jax.ShapeDtypeStruct((80, 2 * HD), F32),
            jax.ShapeDtypeStruct((16, 2 * HD), F32),
            jax.ShapeDtypeStruct((2, 8, 384), F32),
        ),
        in_specs=[smem, smem, smem, vm, pl.BlockSpec(memory_space=pl.ANY)],
        out_specs=(vm, vm, vm, vm),
        scratch_shapes=[
            pltpu.VMEM((count, 16, HD), BF),
            pltpu.VMEM((count, HD), F32),
            pltpu.VMEM((80, HD), jnp.int32),
            pltpu.SemaphoreType.DMA((count,)),
        ],
        name="prepare",
    )(new_ids.T, page_order, lengths, freq, embedding)


def rope(values, cosine, sine):
    return values * cosine + pltpu.roll(values, HD // 2, 1) * sine


def coded(column):
    lane = lax.broadcasted_iota(jnp.int32, (column.shape[0], HD), 1)
    wide = jnp.broadcast_to(column, lane.shape)
    high = wide.astype(BF).astype(F32)
    middle = (wide - high).astype(BF).astype(F32)
    low = wide - high - middle
    parts = jnp.where(lane == 0, high, jnp.where(lane == 1, middle, jnp.where(lane == 2, low, 0.0)))
    line16 = lax.broadcasted_iota(jnp.int32, (16, HD), 0)
    lane16 = lax.broadcasted_iota(jnp.int32, (16, HD), 1)
    first = (line16 == lane16).astype(F32).astype(BF)
    return lax.dot_general(
        first, parts.astype(BF), (((1,), (1,)), ((), ())), preferred_element_type=F32
    ).astype(BF)


def decoded(rows):
    line16 = lax.broadcasted_iota(jnp.int32, (16, HD), 0)
    ones = jnp.where(line16 < 3, 1.0, 0.0).astype(BF)
    return lax.dot_general(
        rows, ones, (((0,), (0,)), ((), ())), preferred_element_type=F32
    )


def merged(blocks):
    levels = [decoded(b[128:144]) for b in blocks]
    peak = functools.reduce(jnp.maximum, levels)
    weights = [jnp.exp(level - peak) for level in levels]
    total = functools.reduce(jnp.add, weights)
    summed = functools.reduce(
        jnp.add, [w * b[0:128].astype(F32) for w, b in zip(weights, blocks)]
    )
    return summed / total, (peak + jnp.log(total))[:, 0:1]


STEPS = (
    (0, 0), (1, 0), (2, 0), (0, 1), (0, 2), (1, 1), (1, 2), (3, 0),
    (2, 1), (2, 2), (3, 1), (3, 2), (0, 3), (1, 3), (2, 3), (3, 3),
)
PART1 = (1, 3, 5, 7)
PART2 = (9, 10, 11, 12)


def pick_int(n, values):
    found = jnp.int32(values[0])
    for j in range(1, len(values)):
        found = jnp.where(n == j, jnp.int32(values[j]), found)
    return found


def offset_of(k):
    return k // 2 + 3 * (k % 2) - 2 * (k // 3)


def main_kernel(
    hid, down, picked, qproj, ku, vu, outp, page, bias, ftab,
    out_ref,
    H, W, acc, QP, OP, kub, vub, tabs, ppage, pbias, pickb, part, rcore, qsum, rz, ry, rx, qz,
    Bm, FK, FV, Q, ob, lev, cz, cmine, cy, cx, fin,
    lsem, wl, hs, hr, ws, wr, xs, ps, pr, fs, fr, es, er,
):
    s, y, x, c, z = [lax.axis_index(a) for a in AXES]
    o = 1 - c

    def dev(s_=s, y_=y, x_=x, c_=c, z_=z):
        return (s_, y_, x_, c_, z_)

    core_dev = dev(c_=o)
    pair_dev = dev(s_=1 - s)
    cross_dev = dev(s_=1 - s, x_=1 - x)
    xhi_dev = dev(x_=1 - x)
    z_dev = [dev(z_=lax.rem(z + d, 4)) for d in (1, 2, 3)]
    y_dev = [dev(y_=lax.rem(y + d, 4)) for d in (1, 2, 3)]

    def remote(src, dst, send, recv, device):
        return pltpu.make_async_remote_copy(
            src_ref=src, dst_ref=dst, send_sem=send, recv_sem=recv,
            device_id=device, device_id_type=MESH,
        )

    own_rows = pl.ds(pl.multiple_of(c * 128, 128), 128)
    w_local = []
    for i in range(4):
        mine = pl.ds(pl.multiple_of((2 * i + c) * 128, 128), 128)
        copy = pltpu.make_async_copy(
            down.at[:, mine], W.at[x, y, z, own_rows, pl.ds(i * 128, 128)], wl.at[i]
        )
        copy.start()
        w_local.append(copy)
    qcopy = pltpu.make_async_copy(qproj, QP, lsem.at[4])
    qcopy.start()

    everyone = [core_dev, pair_dev, cross_dev, xhi_dev, dev(x_=1 - x, c_=o)] + z_dev + y_dev
    barrier = pltpu.get_barrier_semaphore()
    for device in everyone:
        pl.semaphore_signal(barrier, inc=1, device_id=device, device_id_type=MESH)
    pl.semaphore_wait(barrier, len(everyone))

    sent = []

    def go(copy):
        copy.start()
        sent.append(copy)
        return copy

    ex = [0]

    def message(src, dst, device):
        k = ex[0]
        ex[0] += 1
        return remote(src, dst, es.at[k], er.at[k], device)

    m_pick = go(message(picked, pickb, pair_dev))
    w_init = []
    for i in range(4):
        theirs = pl.ds(pl.multiple_of((2 * i + o) * 128, 128), 128)
        w_init.append(go(remote(
            down.at[:, theirs], W.at[x, y, z, own_rows, pl.ds(i * 128, 128)],
            ws.at[i], wr.at[i], core_dev,
        )))
    def ychunk(q):
        yy = lax.rem(y + (0, 3, 1, 2)[q], 4)
        return pl.ds(pl.multiple_of(yy * 2048, 2048), 2048)

    hlocal = [
        pltpu.make_async_copy(hid.at[:, ychunk(q)], H.at[0, :, ychunk(q)], lsem.at[q])
        for q in range(4)
    ]
    ocopy = pltpu.make_async_copy(outp, OP, lsem.at[5])

    hremote = [
        remote(hid.at[:, ychunk(q)], H.at[1, :, ychunk(q)], hs.at[q], hr.at[q], core_dev)
        for q in range(4)
    ]
    m_kv = [go(message(ku.at[c], kub.at[z], z_dev[d])) for d in range(3)]
    m_kv += [go(message(vu.at[c], vub.at[z], z_dev[d])) for d in range(3)]

    in_plane = pl.ds(pl.multiple_of(s * 64, 64), 192)
    prow = pl.ds(pl.multiple_of(s * 224, 32), 32)
    crow = pl.ds(pl.multiple_of(32 + s * 160, 32), 32)
    ia = z * o + y * c
    ib = y * o + z * c

    def place(a_off, b_off):
        a_at = lax.rem(ia + a_off, 4)
        b_at = lax.rem(ib + b_off, 4)
        return (b_at * o + a_at * c, a_at * o + b_at * c)

    def unit(u):
        return x + u - 2 * x * u

    def a_dev(step):
        return dev(y_=lax.rem(y + step * c, 4), z_=lax.rem(z + step * o, 4))

    def b_dev(step):
        return dev(y_=lax.rem(y + step * o, 4), z_=lax.rem(z + step * c, 4))

    def piece(line, m, along_a, a_off):
        u = (0, 1, 0, 1, 0, 1)[m]
        step = (1, 1, 3, 3, 1, 3)[m]
        off = (0, 0, 0, 0, 3, 1)[m]
        if along_a:
            at = place(off, 0)
            device = a_dev(step)
        else:
            at = place(a_off, off)
            device = b_dev(step)
        ref = W.at[unit(u), at[0], at[1], in_plane]
        return remote(ref, ref, ps.at[line, m], pr.at[line, m], device)

    def a_piece(m):
        return piece(4, m, True, None)

    def b_piece(k, m):
        return piece(k, m, False, offset_of(k))

    def side_piece(k, b, which):
        at = place(offset_of(k), offset_of(b))
        rows = prow if which == 0 else crow
        ref = W.at[:, at[0], at[1], rows]
        return remote(
            ref, ref, fs.at[k, b, which], fr.at[k, b, which], pair_dev if which == 0 else cross_dev
        )

    def side_start(k, b):
        side_piece(k, b, 0).start()
        side_piece(k, b, 1).start()

    for copy in w_local:
        copy.wait()
    for copy in w_init:
        copy.wait_recv()
    own = W.at[x, y, z]
    m_cross = go(remote(own, own, xs.at[0], xs.at[1], cross_dev))
    for m in (0, 2):
        a_piece(m).start()
        b_piece(0, m).start()
    for q in (0, 1):
        go(hremote[q])
    for copy in hlocal:
        copy.start()
    ocopy.start()

    m_pick.wait_recv()
    both = (picked[...].astype(F32) + pickb[...].astype(F32)).astype(BF)
    pickb[...] = both
    rows16 = pickb[pl.ds(pl.multiple_of(s * 16, 16), 16), :]
    wide16 = rows16.astype(F32)
    squares = wide16 * wide16
    qcopy.wait()
    for cc in (0, 1):
        for i in range(4):
            g = 2 * i + cc
            part[cc, i, :, 0:1024] = jnp.dot(
                rows16, QP[:, g * 1024 : (g + 1) * 1024], preferred_element_type=F32
            )
            part[cc, i, :, 1024:1152] = jnp.dot(
                rows16, down[:, g * 128 : (g + 1) * 128], preferred_element_type=F32
            )
            part[cc, i, :, 1152:1280] = squares
    m_core = go(message(part.at[o], rcore, core_dev))
    m_tab = go(message(page, ppage, core_dev))
    m_bias = go(message(bias.at[1], pbias, core_dev))
    for q in (2, 3):
        go(hremote[q])

    m_cross.wait_recv()
    for m in (1, 3):
        a_piece(m).start()
        b_piece(0, m).start()

    a_piece(0).wait_recv()
    a_piece(4).start()
    b_piece(1, 0).start()
    b_piece(1, 2).start()
    a_piece(2).wait_recv()

    m_core.wait_recv()
    for i in range(4):
        qsum[i] = part[c, i] + rcore[i]
    m_z = [
        go(message(qsum.at[lax.rem(z + d, 4)], rz.at[d - 1], z_dev[d - 1])) for d in (1, 2, 3)
    ]

    a_piece(1).wait_recv()
    b_piece(1, 1).start()
    b_piece(1, 3).start()
    side_start(1, 0)
    a_piece(3).wait_recv()
    a_piece(5).start()
    side_start(2, 0)

    for m in m_z:
        m.wait_recv()
    rz[3] = qsum[z] + rz[0] + rz[1] + rz[2]
    m_y = [go(message(rz.at[3], ry.at[d - 1], y_dev[d - 1])) for d in (1, 2, 3)]

    for m in m_y:
        m.wait_recv()
    ry[3] = rz[3] + ry[0] + ry[1] + ry[2]
    m_x = go(message(ry.at[3], rx, xhi_dev))

    lines = [st[0] for st in STEPS]
    places = [st[1] for st in STEPS]

    m_q = [message(qz.at[z], qz.at[z], z_dev[d - 1]) for d in (1, 2, 3)]
    sent.extend(m_q)

    line = lax.broadcasted_iota(jnp.int32, (128, 128), 0)
    lane = lax.broadcasted_iota(jnp.int32, (128, 128), 1)
    lane16 = lax.broadcasted_iota(jnp.int32, (16, 128), 1)

    def step(n, carry):
        for k in range(4):
            @pl.when(n == PART1[k])
            def _():
                b_piece(k, 0).wait_recv()
                b_piece(k, 4).start()
                b_piece(k, 3).wait_recv()
                b_piece(k, 5).start()
                b_piece(k, 1).wait_recv()
                side_start(k, 1)
                b_piece(k, 2).wait_recv()
                side_start(k, 2)
                if k == 0:
                    a_piece(4).wait_recv()
                    a_piece(5).wait_recv()
                    side_start(3, 0)
                if k < 2:
                    for m in range(4):
                        b_piece(k + 2, m).start()

            @pl.when(n == PART2[k])
            def _():
                b_piece(k, 4).wait_recv()
                b_piece(k, 5).wait_recv()
                side_start(k, 3)

        @pl.when(n == 1)
        def _():
            m_x.wait_recv()
            total = ry[3] + rx[...]
            inverse = lax.rsqrt(
                jnp.sum(total[:, 1152:1280], axis=1, keepdims=True) / D + 1e-05
            )
            cosine = ftab[:, 0:128]
            sine = ftab[:, 128:256]
            for j in range(8):
                head = total[:, j * 128 : (j + 1) * 128] * inverse
                qz[z, :, j * 128 : (j + 1) * 128] = rope(head, cosine, sine).astype(BF)
            qz[z, :, 1024:1152] = (total[:, 1024:1152] * inverse).astype(BF)
            for m in m_q:
                m.start()

        @pl.when(n == 4)
        def _():
            m_tab.wait_recv()
            m_bias.wait_recv()
            pbias[...] = pbias[...] + bias[0]
            cos_b = page[64:80, 0:HD]
            sin_b = page[64:80, HD : 2 * HD]
            sign = jnp.where(lane16 < HD // 2, -1.0, 1.0)
            for t in range(2):
                ref = ppage if t else page
                for p in range(48):
                    cos_a = ref[p : p + 1, 0:HD]
                    sin_a = ref[p : p + 1, HD : 2 * HD]
                    tabs[t, p * 16 : (p + 1) * 16, 0:HD] = cos_a * cos_b - sin_a * sin_b
                    tabs[t, p * 16 : (p + 1) * 16, HD : 2 * HD] = (
                        sin_a * cos_b + cos_a * sin_b
                    ) * sign

        @pl.when(n == 8)
        def _():
            for m in m_kv:
                m.wait_recv()
            kub[z] = ku[c]
            vub[z] = vu[c]
            for m in m_q:
                m.wait_recv()
            to_requests = (
                lane == (line % 32) // 4 * 16 + line // 32 * 4 + line % 4
            ).astype(F32).astype(BF)
            pad = jnp.zeros((112, 128), BF)
            for i in range(4):
                Bm[i] = jnp.zeros((128, 256), BF)
                Bm[i, 0:64, 0:128] = kub[i]
                Bm[i, 64:128, 128:256] = vub[i]
                heads = jnp.concatenate(
                    [qz[i, :, j * 128 : (j + 1) * 128] for j in range(8)], axis=0
                )
                Q[i] = jnp.dot(to_requests, heads, preferred_element_type=F32).astype(BF)
                fresh = jnp.dot(qz[i, :, 1024:1152], Bm[i], preferred_element_type=F32)
                FK[i] = jnp.concatenate(
                    [rope(fresh[:, 0:128], ftab[:, 0:128], ftab[:, 128:256]).astype(BF), pad],
                    axis=0,
                )
                FV[i] = jnp.concatenate([fresh[:, 128:256].astype(BF), pad], axis=0)

        for q, at in enumerate((0, 1, 2, 7)):
            @pl.when(n == at)
            def _():
                hlocal[q].wait()
                hremote[q].wait_recv()

        k = pick_int(n, lines)
        b = pick_int(n, places)

        @pl.when(n > 0)
        def _():
            side_piece(k, b, 0).wait_recv()
            side_piece(k, b, 1).wait_recv()

        yy, zz = place(offset_of(k), offset_of(b))

        def columns(xh, core):
            return pl.ds(pl.multiple_of((((yy * 2 + xh) * 2 + core) * 4 + zz) * 128, 128), 128)

        def tile(t, carry):
            left = [
                jnp.concatenate([H[t, :, columns(xh, 0)], H[t, :, columns(xh, 1)]], axis=1)
                for xh in (0, 1)
            ]
            product = jnp.dot(left[0], W[0, yy, zz], preferred_element_type=F32) + jnp.dot(
                left[1], W[1, yy, zz], preferred_element_type=F32
            )

            @pl.when(n == 0)
            def _():
                acc[t] = product

            @pl.when(n > 0)
            def _():
                acc[t] += product

            return carry

        lax.fori_loop(0, 2, tile, 0)
        return carry

    lax.fori_loop(0, 16, step, 0)

    elsewhere = jnp.where((y + x + z) == 0, 0.0, masked_score)
    row32 = lax.broadcasted_iota(jnp.int32, (32, 128), 0)
    col32 = lax.broadcasted_iota(jnp.int32, (32, 128), 1)
    scaling = 1.0 / math.sqrt(HD)

    def request(r, carry):
        rows = pl.ds(pl.multiple_of(r * 192, 64), 192)
        cosine = jnp.concatenate([tabs[0, rows, 0:128], tabs[1, rows, 0:128]], axis=0)
        sine = jnp.concatenate([tabs[0, rows, 128:256], tabs[1, rows, 128:256]], axis=0)
        seen = (col32 // 4 == r) & (col32 % 4 <= row32 % 4)
        mask = jnp.concatenate(
            [
                jnp.broadcast_to(pbias[pl.ds(r, 1), :], (32, 384)),
                jnp.where(seen, elsewhere, masked_score),
            ],
            axis=1,
        )
        for i in range(4):
            latent = jnp.concatenate(
                [acc[0, rows, i * 128 : (i + 1) * 128], acc[1, rows, i * 128 : (i + 1) * 128]],
                axis=0,
            ).astype(BF)
            rebuilt = jnp.dot(latent, Bm[i], preferred_element_type=F32)
            keys = jnp.concatenate(
                [rope(rebuilt[:, 0:128], cosine, sine).astype(BF), FK[i]], axis=0
            )
            values = jnp.concatenate([rebuilt[:, 128:256].astype(BF), FV[i]], axis=0)
            query = Q[i, pl.ds(pl.multiple_of(r * 32, 32), 32), :]
            scores = lax.dot_general(
                query, keys, (((1,), (1,)), ((), ())), preferred_element_type=F32
            ) * scaling + mask
            peak = jnp.max(scores, axis=1, keepdims=True)
            e = jnp.where(mask > -1e29, jnp.exp(scores - peak), 0.0)
            total = jnp.sum(e, axis=1, keepdims=True)
            context = jnp.dot(e.astype(BF), values, preferred_element_type=F32)
            some = total > 0.0
            safe = jnp.where(some, total, 1.0)
            level = jnp.where(some, peak + jnp.log(safe), masked_score)
            at = pl.ds(pl.multiple_of(r * 32, 32), 32)
            ob[i, at, 0:128] = (context / safe).astype(BF)
            lev[i, at, :] = jnp.broadcast_to(level, (32, HD))
        return carry

    lax.fori_loop(0, 4, request, 0)

    for i in range(4):
        ob[i, 128:144, :] = coded(lev[i, :, 0:1])
    m_cz = [
        go(message(ob.at[lax.rem(z + d, 4)], cz.at[d - 1], z_dev[d - 1])) for d in (1, 2, 3)
    ]
    for m in m_cz:
        m.wait_recv()
    value, level = merged([ob[z], cz[0], cz[1], cz[2]])
    cmine[0:128] = value.astype(BF)
    cmine[128:144] = coded(level)
    m_cy = [go(message(cmine, cy.at[d - 1], y_dev[d - 1])) for d in (1, 2, 3)]
    for m in m_cy:
        m.wait_recv()
    value, level = merged([cmine[...], cy[0], cy[1], cy[2]])
    cx[c, x, 0:128] = value.astype(BF)
    cx[c, x, 128:144] = coded(level)
    slot = cx.at[c, x]
    m_cx = [go(message(slot, slot, device)) for device in (xhi_dev, core_dev, dev(x_=1 - x, c_=o))]
    for m in m_cx:
        m.wait_recv()
    ocopy.wait()
    to_heads = (
        lane == (line % 16) // 4 * 32 + line // 16 * 4 + line % 4
    ).astype(F32).astype(BF)
    heads = []
    for g in range(2):
        value, _ = merged([cx[g, 0], cx[g, 1]])
        moved = jnp.dot(to_heads, value.astype(BF), preferred_element_type=F32).astype(BF)
        heads += [moved[j * 16 : (j + 1) * 16] for j in range(8)]
    fin[z] = jnp.dot(
        jnp.concatenate(heads, axis=1), OP[...], preferred_element_type=F32
    ).astype(BF)
    m_fin = [go(message(fin.at[z], fin.at[z], z_dev[d - 1])) for d in (1, 2, 3)]
    for m in m_fin:
        m.wait_recv()
    result = functools.reduce(jnp.add, [fin[d].astype(F32) for d in range(4)])
    for r in range(4):
        out_ref[r] = result[r * 4 : (r + 1) * 4].astype(BF)

    for copy in sent:
        copy.wait_send()
    for m in range(6):
        a_piece(m).wait_send()

    def drain(k, carry):
        for m in range(6):
            b_piece(k, m).wait_send()
        for b in range(4):
            @pl.when(k + b > 0)
            def _():
                side_piece(k, b, 0).wait_send()
                side_piece(k, b, 1).wait_send()
        return carry

    lax.fori_loop(0, 4, drain, 0)


MESSAGES = 1 + 6 + 3 + 3 + 3 + 1 + 3 + 3 + 3 + 3 + 3


def main(hid, down, picked, qproj, ku, vu, outp, page, bias, ftab):
    vm = pl.BlockSpec(memory_space=pltpu.VMEM)
    anyspace = pl.BlockSpec(memory_space=pl.ANY)
    V = pltpu.VMEM
    S = pltpu.SemaphoreType.DMA
    return pl.pallas_call(
        main_kernel,
        out_shape=jax.ShapeDtypeStruct((4, 4, 512), BF),
        in_specs=[anyspace, vm, vm, anyspace, vm, vm, anyspace, vm, vm, vm],
        out_specs=vm,
        scratch_shapes=[
            V((2, 768, 8192), BF),
            V((2, 4, 4, 256, 512), BF),
            V((2, 768, 512), F32),
            V((128, 8192), BF),
            V((2048, 512), BF),
            V((4, 64, 128), BF),
            V((4, 64, 128), BF),
            V((2, 768, 256), F32),
            V((80, 256), F32),
            V((8, 384), F32),
            V((32, 128), BF),
            V((2, 4, 16, 1280), F32),
            V((4, 16, 1280), F32),
            V((4, 16, 1280), F32),
            V((4, 16, 1280), F32),
            V((4, 16, 1280), F32),
            V((16, 1280), F32),
            V((4, 16, 1152), BF),
            V((4, 128, 256), BF),
            V((4, 128, 128), BF),
            V((4, 128, 128), BF),
            V((4, 128, 128), BF),
            V((4, 144, 128), BF),
            V((4, 128, 128), F32),
            V((3, 144, 128), BF),
            V((144, 128), BF),
            V((3, 144, 128), BF),
            V((2, 2, 144, 128), BF),
            V((4, 16, 512), BF),
            S((6,)),
            S((4,)),
            S((4,)),
            S((4,)),
            S((4,)),
            S((4,)),
            S((2,)),
            S((5, 6)),
            S((5, 6)),
            S((4, 4, 2)),
            S((4, 4, 2)),
            S((MESSAGES,)),
            S((MESSAGES,)),
        ],
        compiler_params=pltpu.CompilerParams(
            collective_id=0, has_side_effects=True, vmem_limit_bytes=62 * 2**20
        ),
        name="gather_decode",
    )(hid, down, picked, qproj, ku, vu, outp, page, bias, ftab)


def local(
    cached_hidden, page_order, lengths, new_ids, embedding,
    query_proj, down_proj, key_up, value_up, out_proj,
):
    requests, span, width = cached_hidden.shape
    frequency = 1.0 / rope_base ** (np.arange(HD // 2) * 2.0 / HD)
    freq = jnp.asarray(np.tile(np.concatenate([frequency, frequency]), (8, 1)).astype(np.float32))
    picked, page, fresh, bias = prepare(new_ids, page_order, lengths, freq, embedding)
    return main(
        cached_hidden.reshape(requests * span, width), down_proj, picked, query_proj, key_up,
        value_up, out_proj, page, bias, fresh,
    )


def solution(mesh):
    finer = Mesh(
        mesh.devices.reshape(mesh.shape["side"], 4, 2, 2, mesh.shape["head"]), AXES
    )
    placed = (
        P("side", SEQ_HEAD, None),
        P("side", SEQ_HEAD),
        P("side"),
        P(),
        P("side", SEQ_HEAD),
        P(SEQ_HEAD, None),
        P(SEQ_HEAD, None),
        P("head", None, None),
        P("head", None, None),
        P("head", SEQ),
    )
    return jax.shard_map(
        local, mesh=finer, in_specs=placed, out_specs=P("side", None, SEQ), check_vma=False
    )
```

```python
import functools
import math

import jax
import jax.numpy as jnp
import numpy as np
from jax import lax
from jax.experimental import pallas as pl
from jax.experimental.pallas import tpu as pltpu
from jax.sharding import Mesh
from jax.sharding import PartitionSpec as P

D = 8192
HD = 128
PAGE = 16
SEQ = ("seq_0", "seq_1", "seq_2")
SIDE_SEQ_HEAD = ("side", "seq_0", "seq_1", "seq_2", "head")
SEQ_HEAD = ("seq_0", "seq_1", "seq_2", "head")
AXES = ("side", "seq_0", "seq_1", "seq_2", "head")
MESH = pl.DeviceIdType.MESH
rope_base = 500000.0
masked_score = -1e30
BF = jnp.bfloat16
F32 = jnp.float32


def prepare_kernel(
    ids_ref, order_ref, lengths_ref, freq_ref, emb_ref,
    out_ref, page_ref, fresh_ref, bias_ref,
    blocks, rows, line_at, sems,
):
    vocab = emb_ref.shape[0]
    first = lax.axis_index("side") * vocab
    count = blocks.shape[0]
    steps = ids_ref.shape[0]
    requests, pages = order_ref.shape
    span = pages * PAGE
    start = lax.axis_index(SEQ_HEAD) * span
    subs = []
    copies = []
    for i in range(count):
        raw = ids_ref[i % steps, i // steps] - first
        inside = jnp.logical_and(raw >= 0, raw < vocab)
        local = jnp.clip(raw, 0, vocab - 1)
        block = local // 16
        subs.append(jnp.where(inside, local - block * 16, -1))
        copy = pltpu.make_async_copy(
            emb_ref.at[pl.ds(pl.multiple_of(block * 16, 16), 16)], blocks.at[i], sems.at[i]
        )
        copy.start()
        copies.append(copy)
    lane = lax.broadcasted_iota(jnp.int32, (1, 384), 1)
    bias_ref[...] = jnp.zeros_like(bias_ref)
    for r in range(requests):
        at = jnp.zeros((1, 384), jnp.int32)
        for j in range(pages):
            k = order_ref[r, j]
            line_at[pl.ds(r * pages + k, 1), :] = jnp.full((1, HD), start + j * PAGE, jnp.int32)
            at = jnp.where(
                (lane // PAGE) % pages == k, start + j * PAGE + lane % PAGE, at
            )
        dead = jnp.where(at < lengths_ref[r], 0.0, masked_score)
        bias_ref[0, pl.ds(r, 1), :] = jnp.where(lane < span, dead, 0.0)
        bias_ref[1, pl.ds(r, 1), :] = jnp.where(lane >= span, dead, 0.0)
        for t in range(steps):
            line_at[pl.ds(requests * pages + r * steps + t, 1), :] = jnp.full(
                (1, HD), lengths_ref[r] + t, jnp.int32
            )
    offset = lax.broadcasted_iota(jnp.int32, (PAGE, HD), 0)
    line_at[pl.ds(64, PAGE), :] = offset
    angles = line_at[...].astype(F32) * freq_ref[0:1, :]
    cosine = jnp.cos(angles)
    sine = jnp.sin(angles)
    page_ref[:, 0:HD] = cosine
    page_ref[:, HD : 2 * HD] = sine
    half = lax.broadcasted_iota(jnp.int32, (16, HD), 1) < HD // 2
    fresh_ref[:, 0:HD] = cosine[48:64]
    fresh_ref[:, HD : 2 * HD] = jnp.where(half, -sine[48:64], sine[48:64])
    line = lax.broadcasted_iota(jnp.int32, (16, HD), 0)
    for i in range(count):
        copies[i].wait()
        part = jnp.where(line == subs[i], blocks[i].astype(F32), 0.0)
        rows[pl.ds(i, 1), :] = jnp.sum(part, axis=0, keepdims=True)
    out_ref[...] = rows[...].astype(BF)


def prepare(new_ids, page_order, lengths, freq, embedding):
    count = new_ids.size
    smem = pl.BlockSpec(memory_space=pltpu.SMEM)
    vm = pl.BlockSpec(memory_space=pltpu.VMEM)
    return pl.pallas_call(
        prepare_kernel,
        out_shape=(
            jax.ShapeDtypeStruct((count, HD), BF),
            jax.ShapeDtypeStruct((80, 2 * HD), F32),
            jax.ShapeDtypeStruct((16, 2 * HD), F32),
            jax.ShapeDtypeStruct((2, 8, 384), F32),
        ),
        in_specs=[smem, smem, smem, vm, pl.BlockSpec(memory_space=pl.ANY)],
        out_specs=(vm, vm, vm, vm),
        scratch_shapes=[
            pltpu.VMEM((count, 16, HD), BF),
            pltpu.VMEM((count, HD), F32),
            pltpu.VMEM((80, HD), jnp.int32),
            pltpu.SemaphoreType.DMA((count,)),
        ],
        name="prepare",
    )(new_ids.T, page_order, lengths, freq, embedding)


def rope(values, cosine, sine):
    return values * cosine + pltpu.roll(values, HD // 2, 1) * sine


def coded(column):
    lane = lax.broadcasted_iota(jnp.int32, (column.shape[0], HD), 1)
    wide = jnp.broadcast_to(column, lane.shape)
    high = wide.astype(BF).astype(F32)
    middle = (wide - high).astype(BF).astype(F32)
    low = wide - high - middle
    parts = jnp.where(lane == 0, high, jnp.where(lane == 1, middle, jnp.where(lane == 2, low, 0.0)))
    line16 = lax.broadcasted_iota(jnp.int32, (16, HD), 0)
    lane16 = lax.broadcasted_iota(jnp.int32, (16, HD), 1)
    first = (line16 == lane16).astype(F32).astype(BF)
    return lax.dot_general(
        first, parts.astype(BF), (((1,), (1,)), ((), ())), preferred_element_type=F32
    ).astype(BF)


def decoded(rows):
    line16 = lax.broadcasted_iota(jnp.int32, (16, HD), 0)
    ones = jnp.where(line16 < 3, 1.0, 0.0).astype(BF)
    return lax.dot_general(
        rows, ones, (((0,), (0,)), ((), ())), preferred_element_type=F32
    )


def merged(blocks):
    levels = [decoded(b[128:144]) for b in blocks]
    peak = functools.reduce(jnp.maximum, levels)
    weights = [jnp.exp(level - peak) for level in levels]
    total = functools.reduce(jnp.add, weights)
    summed = functools.reduce(
        jnp.add, [w * b[0:128].astype(F32) for w, b in zip(weights, blocks)]
    )
    return summed / total, (peak + jnp.log(total))[:, 0:1]


STEPS = (
    (0, 0), (1, 0), (2, 0), (0, 1), (0, 2), (1, 1), (1, 2), (3, 0),
    (0, 3), (2, 1), (2, 2), (1, 3), (3, 1), (3, 2), (2, 3), (3, 3),
)
PART1 = (1, 3, 5, 7)
PART2 = (5, 7, 9, 10)


def pick_int(n, values):
    found = jnp.int32(values[0])
    for j in range(1, len(values)):
        found = jnp.where(n == j, jnp.int32(values[j]), found)
    return found


def offset_of(k):
    return k // 2 + 3 * (k % 2) - 2 * (k // 3)


def main_kernel(
    hid, down, picked, qproj, ku, vu, outp, page, bias, ftab,
    out_ref,
    H, W, acc, QP, OP, kub, vub, tabs, ppage, pbias, pickb, part, rcore, qsum, rz, ry, rx, qz,
    Bm, FK, FV, Q, ob, lev, cz, cmine, cy, cx, fin,
    lsem, wl, hs, hr, ws, wr, xs, ps, pr, fs, fr, es, er,
):
    s, y, x, c, z = [lax.axis_index(a) for a in AXES]
    o = 1 - c

    def dev(s_=s, y_=y, x_=x, c_=c, z_=z):
        return (s_, y_, x_, c_, z_)

    core_dev = dev(c_=o)
    pair_dev = dev(s_=1 - s)
    cross_dev = dev(s_=1 - s, x_=1 - x)
    xhi_dev = dev(x_=1 - x)
    z_dev = [dev(z_=lax.rem(z + d, 4)) for d in (1, 2, 3)]
    y_dev = [dev(y_=lax.rem(y + d, 4)) for d in (1, 2, 3)]

    def remote(src, dst, send, recv, device):
        return pltpu.make_async_remote_copy(
            src_ref=src, dst_ref=dst, send_sem=send, recv_sem=recv,
            device_id=device, device_id_type=MESH,
        )

    own_rows = pl.ds(pl.multiple_of(c * 128, 128), 128)
    w_local = []
    for i in range(4):
        mine = pl.ds(pl.multiple_of((2 * i + c) * 128, 128), 128)
        copy = pltpu.make_async_copy(
            down.at[:, mine], W.at[x, y, z, own_rows, pl.ds(i * 128, 128)], wl.at[i]
        )
        copy.start()
        w_local.append(copy)
    qcopy = pltpu.make_async_copy(qproj, QP, lsem.at[4])
    qcopy.start()

    everyone = [core_dev, pair_dev, cross_dev, xhi_dev, dev(x_=1 - x, c_=o)] + z_dev + y_dev
    barrier = pltpu.get_barrier_semaphore()
    for device in everyone:
        pl.semaphore_signal(barrier, inc=1, device_id=device, device_id_type=MESH)
    pl.semaphore_wait(barrier, len(everyone))

    sent = []

    def go(copy):
        copy.start()
        sent.append(copy)
        return copy

    ex = [0]

    def message(src, dst, device):
        k = ex[0]
        ex[0] += 1
        return remote(src, dst, es.at[k], er.at[k], device)

    m_pick = go(message(picked, pickb, pair_dev))
    w_init = []
    for i in range(4):
        theirs = pl.ds(pl.multiple_of((2 * i + o) * 128, 128), 128)
        w_init.append(go(remote(
            down.at[:, theirs], W.at[x, y, z, own_rows, pl.ds(i * 128, 128)],
            ws.at[i], wr.at[i], core_dev,
        )))
    def ychunk(q):
        yy = lax.rem(y + (0, 3, 1, 2)[q], 4)
        return pl.ds(pl.multiple_of(yy * 2048, 2048), 2048)

    hlocal = [
        pltpu.make_async_copy(hid.at[:, ychunk(q)], H.at[0, :, ychunk(q)], lsem.at[q])
        for q in range(4)
    ]
    ocopy = pltpu.make_async_copy(outp, OP, lsem.at[5])

    hremote = [
        remote(hid.at[:, ychunk(q)], H.at[1, :, ychunk(q)], hs.at[q], hr.at[q], core_dev)
        for q in range(4)
    ]
    m_kv = [go(message(ku.at[c], kub.at[z], z_dev[d])) for d in range(3)]
    m_kv += [go(message(vu.at[c], vub.at[z], z_dev[d])) for d in range(3)]

    in_plane = pl.ds(pl.multiple_of(s * 64, 64), 192)
    prow = pl.ds(pl.multiple_of(s * 224, 32), 32)
    crow = pl.ds(pl.multiple_of(32 + s * 160, 32), 32)
    ia = z * o + y * c
    ib = y * o + z * c

    def place(a_off, b_off):
        a_at = lax.rem(ia + a_off, 4)
        b_at = lax.rem(ib + b_off, 4)
        return (b_at * o + a_at * c, a_at * o + b_at * c)

    def unit(u):
        return x + u - 2 * x * u

    def a_dev(step):
        return dev(y_=lax.rem(y + step * c, 4), z_=lax.rem(z + step * o, 4))

    def b_dev(step):
        return dev(y_=lax.rem(y + step * o, 4), z_=lax.rem(z + step * c, 4))

    def piece(line, m, along_a, a_off):
        u = (0, 1, 0, 1, 0, 1)[m]
        step = (1, 1, 3, 3, 1, 3)[m]
        off = (0, 0, 0, 0, 3, 1)[m]
        if along_a:
            at = place(off, 0)
            device = a_dev(step)
        else:
            at = place(a_off, off)
            device = b_dev(step)
        ref = W.at[unit(u), at[0], at[1], in_plane]
        return remote(ref, ref, ps.at[line, m], pr.at[line, m], device)

    def a_piece(m):
        return piece(4, m, True, None)

    def b_piece(k, m):
        return piece(k, m, False, offset_of(k))

    def side_piece(k, b, which):
        at = place(offset_of(k), offset_of(b))
        rows = prow if which == 0 else crow
        ref = W.at[:, at[0], at[1], rows]
        return remote(
            ref, ref, fs.at[k, b, which], fr.at[k, b, which], pair_dev if which == 0 else cross_dev
        )

    def side_start(k, b):
        side_piece(k, b, 0).start()
        side_piece(k, b, 1).start()

    acc[...] = jnp.zeros_like(acc)

    for copy in w_local:
        copy.wait()
    for copy in w_init:
        copy.wait_recv()
    own = W.at[x, y, z]
    m_cross = go(remote(own, own, xs.at[0], xs.at[1], cross_dev))
    for m in (0, 2):
        a_piece(m).start()
        b_piece(0, m).start()
    for q in (0, 1):
        go(hremote[q])
    for copy in hlocal:
        copy.start()
    ocopy.start()

    m_pick.wait_recv()
    both = (picked[...].astype(F32) + pickb[...].astype(F32)).astype(BF)
    pickb[...] = both
    rows16 = pickb[pl.ds(pl.multiple_of(s * 16, 16), 16), :]
    wide16 = rows16.astype(F32)
    squares = wide16 * wide16
    qcopy.wait()
    for cc in (0, 1):
        for i in range(4):
            g = 2 * i + cc
            part[cc, i, :, 0:1024] = jnp.dot(
                rows16, QP[:, g * 1024 : (g + 1) * 1024], preferred_element_type=F32
            )
            part[cc, i, :, 1024:1152] = jnp.dot(
                rows16, down[:, g * 128 : (g + 1) * 128], preferred_element_type=F32
            )
            part[cc, i, :, 1152:1280] = squares
    m_core = go(message(part.at[o], rcore, core_dev))
    m_tab = go(message(page, ppage, core_dev))
    m_bias = go(message(bias.at[1], pbias, core_dev))
    for q in (2, 3):
        go(hremote[q])

    a_piece(0).wait_recv()
    a_piece(4).start()
    b_piece(1, 0).start()
    b_piece(1, 2).start()
    a_piece(2).wait_recv()
    b_piece(2, 0).start()
    b_piece(2, 2).start()
    m_cross.wait_recv()
    for m in (1, 3):
        a_piece(m).start()
        b_piece(0, m).start()
    a_piece(1).wait_recv()
    b_piece(1, 1).start()
    b_piece(1, 3).start()
    side_start(1, 0)
    a_piece(3).wait_recv()
    a_piece(5).start()
    side_start(2, 0)

    m_z = [
        message(qsum.at[lax.rem(z + d, 4)], rz.at[d - 1], z_dev[d - 1]) for d in (1, 2, 3)
    ]
    m_y = [message(rz.at[3], ry.at[d - 1], y_dev[d - 1]) for d in (1, 2, 3)]
    m_x = message(ry.at[3], rx, xhi_dev)
    sent.extend(m_z + m_y + [m_x])

    lines = [st[0] for st in STEPS]
    places = [st[1] for st in STEPS]

    m_q = [message(qz.at[z], qz.at[z], z_dev[d - 1]) for d in (1, 2, 3)]
    sent.extend(m_q)

    line = lax.broadcasted_iota(jnp.int32, (128, 128), 0)
    lane = lax.broadcasted_iota(jnp.int32, (128, 128), 1)
    lane16 = lax.broadcasted_iota(jnp.int32, (16, 128), 1)

    def step(n, carry):
        for k in range(4):
            @pl.when(n == PART1[k])
            def _():
                b_piece(k, 0).wait_recv()
                b_piece(k, 4).start()
                b_piece(k, 3).wait_recv()
                b_piece(k, 5).start()
                b_piece(k, 1).wait_recv()
                side_start(k, 1)
                b_piece(k, 2).wait_recv()
                side_start(k, 2)
                if k == 0:
                    b_piece(2, 1).start()
                    b_piece(2, 3).start()
                if k == 1:
                    a_piece(4).wait_recv()
                    b_piece(3, 0).start()
                    b_piece(3, 2).start()
                    a_piece(5).wait_recv()
                    b_piece(3, 1).start()
                    b_piece(3, 3).start()
                    side_start(3, 0)

            @pl.when(n == PART2[k])
            def _():
                b_piece(k, 4).wait_recv()
                b_piece(k, 5).wait_recv()
                side_start(k, 3)

        @pl.when(n == 0)
        def _():
            m_core.wait_recv()
            for i in range(4):
                qsum[i] = part[c, i] + rcore[i]
            for m in m_z:
                m.start()

        @pl.when(n == 2)
        def _():
            for m in m_z:
                m.wait_recv()
            rz[3] = qsum[z] + rz[0] + rz[1] + rz[2]
            for m in m_y:
                m.start()

        @pl.when(n == 4)
        def _():
            for m in m_y:
                m.wait_recv()
            ry[3] = rz[3] + ry[0] + ry[1] + ry[2]
            m_x.start()

        @pl.when(n == 6)
        def _():
            m_x.wait_recv()
            total = ry[3] + rx[...]
            inverse = lax.rsqrt(
                jnp.sum(total[:, 1152:1280], axis=1, keepdims=True) / D + 1e-05
            )
            cosine = ftab[:, 0:128]
            sine = ftab[:, 128:256]
            for j in range(8):
                head = total[:, j * 128 : (j + 1) * 128] * inverse
                qz[z, :, j * 128 : (j + 1) * 128] = rope(head, cosine, sine).astype(BF)
            qz[z, :, 1024:1152] = (total[:, 1024:1152] * inverse).astype(BF)
            for m in m_q:
                m.start()

        @pl.when(n == 8)
        def _():
            m_tab.wait_recv()
            m_bias.wait_recv()
            pbias[...] = pbias[...] + bias[0]
            cos_b = page[64:80, 0:HD]
            sin_b = page[64:80, HD : 2 * HD]
            sign = jnp.where(lane16 < HD // 2, -1.0, 1.0)
            for t in range(2):
                ref = ppage if t else page
                for p in range(48):
                    cos_a = ref[p : p + 1, 0:HD]
                    sin_a = ref[p : p + 1, HD : 2 * HD]
                    tabs[t, p * 16 : (p + 1) * 16, 0:HD] = cos_a * cos_b - sin_a * sin_b
                    tabs[t, p * 16 : (p + 1) * 16, HD : 2 * HD] = (
                        sin_a * cos_b + cos_a * sin_b
                    ) * sign

        @pl.when(n == 11)
        def _():
            for m in m_kv:
                m.wait_recv()
            kub[z] = ku[c]
            vub[z] = vu[c]
            for m in m_q:
                m.wait_recv()
            to_requests = (
                lane == (line % 32) // 4 * 16 + line // 32 * 4 + line % 4
            ).astype(F32).astype(BF)
            pad = jnp.zeros((112, 128), BF)
            for i in range(4):
                Bm[i] = jnp.zeros((128, 256), BF)
                Bm[i, 0:64, 0:128] = kub[i]
                Bm[i, 64:128, 128:256] = vub[i]
                heads = jnp.concatenate(
                    [qz[i, :, j * 128 : (j + 1) * 128] for j in range(8)], axis=0
                )
                Q[i] = jnp.dot(to_requests, heads, preferred_element_type=F32).astype(BF)
                fresh = jnp.dot(qz[i, :, 1024:1152], Bm[i], preferred_element_type=F32)
                FK[i] = jnp.concatenate(
                    [rope(fresh[:, 0:128], ftab[:, 0:128], ftab[:, 128:256]).astype(BF), pad],
                    axis=0,
                )
                FV[i] = jnp.concatenate([fresh[:, 128:256].astype(BF), pad], axis=0)

        for q, at in enumerate((0, 1, 2, 7)):
            @pl.when(n == at)
            def _():
                hlocal[q].wait()
                hremote[q].wait_recv()

        k = pick_int(n, lines)
        b = pick_int(n, places)

        @pl.when(n > 0)
        def _():
            side_piece(k, b, 0).wait_recv()
            side_piece(k, b, 1).wait_recv()

        yy, zz = place(offset_of(k), offset_of(b))

        def columns(xh, core):
            return pl.ds(pl.multiple_of((((yy * 2 + xh) * 2 + core) * 4 + zz) * 128, 128), 128)

        def tile(t, carry):
            left = [
                jnp.concatenate([H[t, :, columns(xh, 0)], H[t, :, columns(xh, 1)]], axis=1)
                for xh in (0, 1)
            ]
            product = jnp.dot(left[0], W[0, yy, zz], preferred_element_type=F32) + jnp.dot(
                left[1], W[1, yy, zz], preferred_element_type=F32
            )

            acc[t] += product
            return carry

        lax.fori_loop(0, 2, tile, 0)
        return carry

    lax.fori_loop(0, 16, step, 0)

    elsewhere = jnp.where((y + x + z) == 0, 0.0, masked_score)
    row32 = lax.broadcasted_iota(jnp.int32, (32, 128), 0)
    col32 = lax.broadcasted_iota(jnp.int32, (32, 128), 1)
    scaling = 1.0 / math.sqrt(HD)

    first_cz = ex[0]
    ex[0] += 3

    def partial_message(step):
        i = lax.rem(z + 1 + step, 4)
        return remote(
            ob.at[i], cz.at[step], es.at[first_cz + step], er.at[first_cz + step], dev(z_=i)
        )

    def group(step, carry):
        i = lax.rem(z + 1 + step, 4)
        lanes = pl.ds(pl.multiple_of(i * 128, 128), 128)
        for r in range(4):
            rows = slice(r * 192, (r + 1) * 192)
            at = slice(r * 32, (r + 1) * 32)
            seen = (col32 // 4 == r) & (col32 % 4 <= row32 % 4)
            mask = jnp.concatenate(
                [
                    jnp.broadcast_to(pbias[r : r + 1, :], (32, 384)),
                    jnp.where(seen, elsewhere, masked_score),
                ],
                axis=1,
            )
            latent = jnp.concatenate([acc[0, rows, lanes], acc[1, rows, lanes]], axis=0).astype(BF)
            rebuilt = jnp.dot(latent, Bm[i], preferred_element_type=F32)
            cosine = jnp.concatenate([tabs[0, rows, 0:128], tabs[1, rows, 0:128]], axis=0)
            sine = jnp.concatenate([tabs[0, rows, 128:256], tabs[1, rows, 128:256]], axis=0)
            keys = jnp.concatenate(
                [rope(rebuilt[:, 0:128], cosine, sine).astype(BF), FK[i]], axis=0
            )
            values = jnp.concatenate([rebuilt[:, 128:256].astype(BF), FV[i]], axis=0)
            scores = lax.dot_general(
                Q[i, at, :], keys, (((1,), (1,)), ((), ())), preferred_element_type=F32
            ) * scaling + mask
            peak = jnp.max(scores, axis=1, keepdims=True)
            e = jnp.where(mask > -1e29, jnp.exp(scores - peak), 0.0)
            total = jnp.sum(e, axis=1, keepdims=True)
            context = jnp.dot(e.astype(BF), values, preferred_element_type=F32)
            some = total > 0.0
            safe = jnp.where(some, total, 1.0)
            level = jnp.where(some, peak + jnp.log(safe), masked_score)
            ob[i, at, :] = (context / safe).astype(BF)
            lev[at, :] = jnp.broadcast_to(level, (32, HD))
        ob[i, 128:144, :] = coded(lev[:, 0:1])

        @pl.when(step < 3)
        def _():
            partial_message(step).start()

        return carry

    lax.fori_loop(0, 4, group, 0)

    m_cz = [partial_message(d) for d in range(3)]
    sent.extend(m_cz)
    for m in m_cz:
        m.wait_recv()
    value, level = merged([ob[z], cz[0], cz[1], cz[2]])
    cmine[0:128] = value.astype(BF)
    cmine[128:144] = coded(level)
    m_cy = [go(message(cmine, cy.at[d - 1], y_dev[d - 1])) for d in (1, 2, 3)]
    for m in m_cy:
        m.wait_recv()
    value, level = merged([cmine[...], cy[0], cy[1], cy[2]])
    cx[c, x, 0:128] = value.astype(BF)
    cx[c, x, 128:144] = coded(level)
    slot = cx.at[c, x]
    m_cx = [go(message(slot, slot, device)) for device in (xhi_dev, core_dev, dev(x_=1 - x, c_=o))]
    for m in m_cx:
        m.wait_recv()
    ocopy.wait()
    to_heads = (
        lane == (line % 16) // 4 * 32 + line // 16 * 4 + line % 4
    ).astype(F32).astype(BF)
    heads = []
    for g in range(2):
        value, _ = merged([cx[g, 0], cx[g, 1]])
        moved = jnp.dot(to_heads, value.astype(BF), preferred_element_type=F32).astype(BF)
        heads += [moved[j * 16 : (j + 1) * 16] for j in range(8)]
    fin[z] = jnp.dot(
        jnp.concatenate(heads, axis=1), OP[...], preferred_element_type=F32
    ).astype(BF)
    m_fin = [go(message(fin.at[z], fin.at[z], z_dev[d - 1])) for d in (1, 2, 3)]
    for m in m_fin:
        m.wait_recv()
    result = functools.reduce(jnp.add, [fin[d].astype(F32) for d in range(4)])
    for r in range(4):
        out_ref[r] = result[r * 4 : (r + 1) * 4].astype(BF)

    for copy in sent:
        copy.wait_send()
    for m in range(6):
        a_piece(m).wait_send()

    def drain(k, carry):
        for m in range(6):
            b_piece(k, m).wait_send()
        for b in range(4):
            @pl.when(k + b > 0)
            def _():
                side_piece(k, b, 0).wait_send()
                side_piece(k, b, 1).wait_send()
        return carry

    lax.fori_loop(0, 4, drain, 0)


MESSAGES = 1 + 6 + 3 + 3 + 3 + 1 + 3 + 3 + 3 + 3 + 3


def main(hid, down, picked, qproj, ku, vu, outp, page, bias, ftab):
    vm = pl.BlockSpec(memory_space=pltpu.VMEM)
    anyspace = pl.BlockSpec(memory_space=pl.ANY)
    V = pltpu.VMEM
    S = pltpu.SemaphoreType.DMA
    return pl.pallas_call(
        main_kernel,
        out_shape=jax.ShapeDtypeStruct((4, 4, 512), BF),
        in_specs=[anyspace, vm, vm, anyspace, vm, vm, anyspace, vm, vm, vm],
        out_specs=vm,
        scratch_shapes=[
            V((2, 768, 8192), BF),
            V((2, 4, 4, 256, 512), BF),
            V((2, 768, 512), F32),
            V((128, 8192), BF),
            V((2048, 512), BF),
            V((4, 64, 128), BF),
            V((4, 64, 128), BF),
            V((2, 768, 256), F32),
            V((80, 256), F32),
            V((8, 384), F32),
            V((32, 128), BF),
            V((2, 4, 16, 1280), F32),
            V((4, 16, 1280), F32),
            V((4, 16, 1280), F32),
            V((4, 16, 1280), F32),
            V((4, 16, 1280), F32),
            V((16, 1280), F32),
            V((4, 16, 1152), BF),
            V((4, 128, 256), BF),
            V((4, 128, 128), BF),
            V((4, 128, 128), BF),
            V((4, 128, 128), BF),
            V((4, 144, 128), BF),
            V((128, 128), F32),
            V((3, 144, 128), BF),
            V((144, 128), BF),
            V((3, 144, 128), BF),
            V((2, 2, 144, 128), BF),
            V((4, 16, 512), BF),
            S((6,)),
            S((4,)),
            S((4,)),
            S((4,)),
            S((4,)),
            S((4,)),
            S((2,)),
            S((5, 6)),
            S((5, 6)),
            S((4, 4, 2)),
            S((4, 4, 2)),
            S((MESSAGES,)),
            S((MESSAGES,)),
        ],
        compiler_params=pltpu.CompilerParams(
            collective_id=0, has_side_effects=True, vmem_limit_bytes=62 * 2**20
        ),
        name="gather_decode",
    )(hid, down, picked, qproj, ku, vu, outp, page, bias, ftab)


def local(
    cached_hidden, page_order, lengths, new_ids, embedding,
    query_proj, down_proj, key_up, value_up, out_proj,
):
    requests, span, width = cached_hidden.shape
    frequency = 1.0 / rope_base ** (np.arange(HD // 2) * 2.0 / HD)
    freq = jnp.asarray(np.tile(np.concatenate([frequency, frequency]), (8, 1)).astype(np.float32))
    picked, page, fresh, bias = prepare(new_ids, page_order, lengths, freq, embedding)
    return main(
        cached_hidden.reshape(requests * span, width), down_proj, picked, query_proj, key_up,
        value_up, out_proj, page, bias, fresh,
    )


def solution(mesh):
    finer = Mesh(
        mesh.devices.reshape(mesh.shape["side"], 4, 2, 2, mesh.shape["head"]), AXES
    )
    placed = (
        P("side", SEQ_HEAD, None),
        P("side", SEQ_HEAD),
        P("side"),
        P(),
        P("side", SEQ_HEAD),
        P(SEQ_HEAD, None),
        P(SEQ_HEAD, None),
        P("head", None, None),
        P("head", None, None),
        P("head", SEQ),
    )
    return jax.shard_map(
        local, mesh=finer, in_specs=placed, out_specs=P("side", None, SEQ), check_vma=False
    )
```

```python
import functools
import math

import jax
import jax.numpy as jnp
import numpy as np
from jax import lax
from jax.experimental import pallas as pl
from jax.experimental.pallas import tpu as pltpu
from jax.sharding import Mesh
from jax.sharding import PartitionSpec as P

D = 8192
HD = 128
PAGE = 16
SEQ = ("seq_0", "seq_1", "seq_2")
SIDE_SEQ_HEAD = ("side", "seq_0", "seq_1", "seq_2", "head")
SEQ_HEAD = ("seq_0", "seq_1", "seq_2", "head")
AXES = ("side", "seq_0", "seq_1", "seq_2", "head")
MESH = pl.DeviceIdType.MESH
rope_base = 500000.0
masked_score = -1e30
BF = jnp.bfloat16
F32 = jnp.float32


def prepare_kernel(
    ids_ref, order_ref, lengths_ref, freq_ref, emb_ref,
    out_ref, page_ref, fresh_ref, bias_ref,
    blocks, rows, line_at, sems,
):
    vocab = emb_ref.shape[0]
    first = lax.axis_index("side") * vocab
    count = blocks.shape[0]
    steps = ids_ref.shape[0]
    requests, pages = order_ref.shape
    span = pages * PAGE
    start = lax.axis_index(SEQ_HEAD) * span
    subs = []
    copies = []
    for i in range(count):
        raw = ids_ref[i % steps, i // steps] - first
        inside = jnp.logical_and(raw >= 0, raw < vocab)
        local = jnp.clip(raw, 0, vocab - 1)
        block = local // 16
        subs.append(jnp.where(inside, local - block * 16, -1))
        copy = pltpu.make_async_copy(
            emb_ref.at[pl.ds(pl.multiple_of(block * 16, 16), 16)], blocks.at[i], sems.at[i]
        )
        copy.start()
        copies.append(copy)
    lane = lax.broadcasted_iota(jnp.int32, (1, 384), 1)
    bias_ref[...] = jnp.zeros_like(bias_ref)
    for r in range(requests):
        at = jnp.zeros((1, 384), jnp.int32)
        for j in range(pages):
            k = order_ref[r, j]
            line_at[pl.ds(r * pages + k, 1), :] = jnp.full((1, HD), start + j * PAGE, jnp.int32)
            at = jnp.where(
                (lane // PAGE) % pages == k, start + j * PAGE + lane % PAGE, at
            )
        dead = jnp.where(at < lengths_ref[r], 0.0, masked_score)
        bias_ref[0, pl.ds(r, 1), :] = jnp.where(lane < span, dead, 0.0)
        bias_ref[1, pl.ds(r, 1), :] = jnp.where(lane >= span, dead, 0.0)
        for t in range(steps):
            line_at[pl.ds(requests * pages + r * steps + t, 1), :] = jnp.full(
                (1, HD), lengths_ref[r] + t, jnp.int32
            )
    offset = lax.broadcasted_iota(jnp.int32, (PAGE, HD), 0)
    line_at[pl.ds(64, PAGE), :] = offset
    angles = line_at[...].astype(F32) * freq_ref[0:1, :]
    cosine = jnp.cos(angles)
    sine = jnp.sin(angles)
    page_ref[:, 0:HD] = cosine
    page_ref[:, HD : 2 * HD] = sine
    half = lax.broadcasted_iota(jnp.int32, (16, HD), 1) < HD // 2
    fresh_ref[:, 0:HD] = cosine[48:64]
    fresh_ref[:, HD : 2 * HD] = jnp.where(half, -sine[48:64], sine[48:64])
    line = lax.broadcasted_iota(jnp.int32, (16, HD), 0)
    for i in range(count):
        copies[i].wait()
        part = jnp.where(line == subs[i], blocks[i].astype(F32), 0.0)
        rows[pl.ds(i, 1), :] = jnp.sum(part, axis=0, keepdims=True)
    out_ref[...] = rows[...].astype(BF)


def prepare(new_ids, page_order, lengths, freq, embedding):
    count = new_ids.size
    smem = pl.BlockSpec(memory_space=pltpu.SMEM)
    vm = pl.BlockSpec(memory_space=pltpu.VMEM)
    return pl.pallas_call(
        prepare_kernel,
        out_shape=(
            jax.ShapeDtypeStruct((count, HD), BF),
            jax.ShapeDtypeStruct((80, 2 * HD), F32),
            jax.ShapeDtypeStruct((16, 2 * HD), F32),
            jax.ShapeDtypeStruct((2, 8, 384), F32),
        ),
        in_specs=[smem, smem, smem, vm, pl.BlockSpec(memory_space=pl.ANY)],
        out_specs=(vm, vm, vm, vm),
        scratch_shapes=[
            pltpu.VMEM((count, 16, HD), BF),
            pltpu.VMEM((count, HD), F32),
            pltpu.VMEM((80, HD), jnp.int32),
            pltpu.SemaphoreType.DMA((count,)),
        ],
        name="prepare",
    )(new_ids.T, page_order, lengths, freq, embedding)


def rope(values, cosine, sine):
    return values * cosine + pltpu.roll(values, HD // 2, 1) * sine


def coded(column):
    lane = lax.broadcasted_iota(jnp.int32, (column.shape[0], HD), 1)
    wide = jnp.broadcast_to(column, lane.shape)
    high = wide.astype(BF).astype(F32)
    middle = (wide - high).astype(BF).astype(F32)
    low = wide - high - middle
    parts = jnp.where(lane == 0, high, jnp.where(lane == 1, middle, jnp.where(lane == 2, low, 0.0)))
    line16 = lax.broadcasted_iota(jnp.int32, (16, HD), 0)
    lane16 = lax.broadcasted_iota(jnp.int32, (16, HD), 1)
    first = (line16 == lane16).astype(F32).astype(BF)
    return lax.dot_general(
        first, parts.astype(BF), (((1,), (1,)), ((), ())), preferred_element_type=F32
    ).astype(BF)


def decoded(rows):
    line16 = lax.broadcasted_iota(jnp.int32, (16, HD), 0)
    ones = jnp.where(line16 < 3, 1.0, 0.0).astype(BF)
    return lax.dot_general(
        rows, ones, (((0,), (0,)), ((), ())), preferred_element_type=F32
    )


def merged(blocks):
    levels = [decoded(b[128:144]) for b in blocks]
    peak = functools.reduce(jnp.maximum, levels)
    weights = [jnp.exp(level - peak) for level in levels]
    total = functools.reduce(jnp.add, weights)
    summed = functools.reduce(
        jnp.add, [w * b[0:128].astype(F32) for w, b in zip(weights, blocks)]
    )
    return summed / total, (peak + jnp.log(total))[:, 0:1]


STEPS = (
    (0, 0), (1, 0), (2, 0), (0, 1), (0, 2), (1, 1), (1, 2), (2, 1),
    (2, 2), (3, 0), (0, 3), (1, 3), (3, 1), (3, 2), (2, 3), (3, 3),
)
PART1 = (1, 3, 5, 7)
PART2 = (7, 9, 10, 12)


def pick_int(n, values):
    found = jnp.int32(values[0])
    for j in range(1, len(values)):
        found = jnp.where(n == j, jnp.int32(values[j]), found)
    return found


def offset_of(k):
    return k // 2 + 3 * (k % 2) - 2 * (k // 3)


def main_kernel(
    hid, down_h, picked_h, qproj, ku, vu, outp, page_h, bias_h, ftab_h,
    out_ref,
    down, picked, page, bias, ftab,
    H, W, acc, QP, OP, kub, vub, tabs, ppage, pbias, pickb, part, rcore, qsum, rz, ry, rx, qz,
    Bm, FK, FV, Q, ob, lev, cz, cmine, cy, cx, fin,
    lsem, wl, hs, hr, ws, wr, xs, ps, pr, fs, fr, es, er,
):
    s, y, x, c, z = [lax.axis_index(a) for a in AXES]
    o = 1 - c

    def dev(s_=s, y_=y, x_=x, c_=c, z_=z):
        return (s_, y_, x_, c_, z_)

    core_dev = dev(c_=o)
    pair_dev = dev(s_=1 - s)
    cross_dev = dev(s_=1 - s, x_=1 - x)
    xhi_dev = dev(x_=1 - x)
    z_dev = [dev(z_=lax.rem(z + d, 4)) for d in (1, 2, 3)]
    y_dev = [dev(y_=lax.rem(y + d, 4)) for d in (1, 2, 3)]

    def remote(src, dst, send, recv, device):
        return pltpu.make_async_remote_copy(
            src_ref=src, dst_ref=dst, send_sem=send, recv_sem=recv,
            device_id=device, device_id_type=MESH,
        )

    everyone = [core_dev, pair_dev, cross_dev, xhi_dev, dev(x_=1 - x, c_=o)] + z_dev + y_dev
    barrier = pltpu.get_barrier_semaphore()
    for device in everyone:
        pl.semaphore_signal(barrier, inc=1, device_id=device, device_id_type=MESH)

    own_rows = pl.ds(pl.multiple_of(c * 128, 128), 128)
    w_local = []
    for i in range(4):
        mine = pl.ds(pl.multiple_of((2 * i + c) * 128, 128), 128)
        copy = pltpu.make_async_copy(
            down_h.at[:, mine], W.at[x, y, z, own_rows, pl.ds(i * 128, 128)], wl.at[i]
        )
        copy.start()
        w_local.append(copy)
    small = [
        pltpu.make_async_copy(src, dst, lsem.at[6 + k])
        for k, (src, dst) in enumerate(
            [
                (picked_h, picked), (down_h, down), (ftab_h, ftab), (page_h, page),
                (bias_h, bias), (ku.at[c], kub.at[z]), (vu.at[c], vub.at[z]),
            ]
        )
    ]
    for copy in small:
        copy.start()
    qcopy = pltpu.make_async_copy(qproj, QP, lsem.at[4])
    qcopy.start()

    pl.semaphore_wait(barrier, len(everyone))

    sent = []

    def go(copy):
        copy.start()
        sent.append(copy)
        return copy

    ex = [0]

    def message(src, dst, device):
        k = ex[0]
        ex[0] += 1
        return remote(src, dst, es.at[k], er.at[k], device)

    m_pick = go(message(picked_h, pickb, pair_dev))
    w_init = []
    for i in range(4):
        theirs = pl.ds(pl.multiple_of((2 * i + o) * 128, 128), 128)
        w_init.append(go(remote(
            down_h.at[:, theirs], W.at[x, y, z, own_rows, pl.ds(i * 128, 128)],
            ws.at[i], wr.at[i], core_dev,
        )))
    def ychunk(q):
        yy = lax.rem(y + (0, 3, 1, 2)[q], 4)
        return pl.ds(pl.multiple_of(yy * 2048, 2048), 2048)

    hlocal = [
        pltpu.make_async_copy(hid.at[:, ychunk(q)], H.at[0, :, ychunk(q)], lsem.at[q])
        for q in range(4)
    ]
    ocopy = pltpu.make_async_copy(outp, OP, lsem.at[5])

    hremote = [
        remote(hid.at[:, ychunk(q)], H.at[1, :, ychunk(q)], hs.at[q], hr.at[q], core_dev)
        for q in range(4)
    ]
    m_kv = [go(message(ku.at[c], kub.at[z], z_dev[d])) for d in range(3)]
    m_kv += [go(message(vu.at[c], vub.at[z], z_dev[d])) for d in range(3)]

    in_plane = pl.ds(pl.multiple_of(s * 64, 64), 192)
    prow = pl.ds(pl.multiple_of(s * 224, 32), 32)
    crow = pl.ds(pl.multiple_of(32 + s * 160, 32), 32)
    ia = z * o + y * c
    ib = y * o + z * c

    def place(a_off, b_off):
        a_at = lax.rem(ia + a_off, 4)
        b_at = lax.rem(ib + b_off, 4)
        return (b_at * o + a_at * c, a_at * o + b_at * c)

    def unit(u):
        return x + u - 2 * x * u

    def a_dev(step):
        return dev(y_=lax.rem(y + step * c, 4), z_=lax.rem(z + step * o, 4))

    def b_dev(step):
        return dev(y_=lax.rem(y + step * o, 4), z_=lax.rem(z + step * c, 4))

    def piece(line, m, along_a, a_off):
        u = (0, 1, 0, 1, 0, 1)[m]
        step = (1, 1, 3, 3, 1, 3)[m]
        off = (0, 0, 0, 0, 3, 1)[m]
        if along_a:
            at = place(off, 0)
            device = a_dev(step)
        else:
            at = place(a_off, off)
            device = b_dev(step)
        ref = W.at[unit(u), at[0], at[1], in_plane]
        return remote(ref, ref, ps.at[line, m], pr.at[line, m], device)

    def a_piece(m):
        return piece(4, m, True, None)

    def b_piece(k, m):
        return piece(k, m, False, offset_of(k))

    def side_piece(k, b, which):
        at = place(offset_of(k), offset_of(b))
        rows = prow if which == 0 else crow
        ref = W.at[:, at[0], at[1], rows]
        return remote(
            ref, ref, fs.at[k, b, which], fr.at[k, b, which], pair_dev if which == 0 else cross_dev
        )

    def side_start(k, b):
        side_piece(k, b, 0).start()
        side_piece(k, b, 1).start()

    acc[...] = jnp.zeros_like(acc)

    for copy in w_local:
        copy.wait()
    for copy in w_init:
        copy.wait_recv()
    own = W.at[x, y, z]
    m_cross = go(remote(own, own, xs.at[0], xs.at[1], cross_dev))
    for m in (0, 2):
        a_piece(m).start()
        b_piece(0, m).start()
    for q in (0, 1):
        go(hremote[q])
    for copy in hlocal:
        copy.start()
    ocopy.start()

    m_pick.wait_recv()
    small[0].wait()
    small[1].wait()
    both = (picked[...].astype(F32) + pickb[...].astype(F32)).astype(BF)
    pickb[...] = both
    rows16 = pickb[pl.ds(pl.multiple_of(s * 16, 16), 16), :]
    wide16 = rows16.astype(F32)
    squares = wide16 * wide16
    qcopy.wait()
    for cc in (0, 1):
        for i in range(4):
            g = 2 * i + cc
            part[cc, i, :, 0:1024] = jnp.dot(
                rows16, QP[:, g * 1024 : (g + 1) * 1024], preferred_element_type=F32
            )
            part[cc, i, :, 1024:1152] = jnp.dot(
                rows16, down[:, g * 128 : (g + 1) * 128], preferred_element_type=F32
            )
            part[cc, i, :, 1152:1280] = squares
    m_core = go(message(part.at[o], rcore, core_dev))
    m_tab = go(message(page_h, ppage, core_dev))
    m_bias = go(message(bias_h.at[1], pbias, core_dev))
    for q in (2, 3):
        go(hremote[q])

    a_piece(0).wait_recv()
    a_piece(4).start()
    b_piece(1, 0).start()
    b_piece(1, 2).start()
    a_piece(2).wait_recv()
    b_piece(2, 0).start()
    b_piece(2, 2).start()
    b_piece(0, 0).wait_recv()
    b_piece(0, 4).start()
    m_cross.wait_recv()
    for m in (1, 3):
        a_piece(m).start()
        b_piece(0, m).start()

    m_z = [
        message(qsum.at[lax.rem(z + d, 4)], rz.at[d - 1], z_dev[d - 1]) for d in (1, 2, 3)
    ]
    m_y = [message(rz.at[3], ry.at[d - 1], y_dev[d - 1]) for d in (1, 2, 3)]
    m_x = message(ry.at[3], rx, xhi_dev)
    sent.extend(m_z + m_y + [m_x])

    lines = [st[0] for st in STEPS]
    places = [st[1] for st in STEPS]

    m_q = [message(qz.at[z], qz.at[z], z_dev[d - 1]) for d in (1, 2, 3)]
    sent.extend(m_q)

    line = lax.broadcasted_iota(jnp.int32, (128, 128), 0)
    lane = lax.broadcasted_iota(jnp.int32, (128, 128), 1)
    lane16 = lax.broadcasted_iota(jnp.int32, (16, 128), 1)

    def step(n, carry):
        @pl.when(n == 1)
        def _():
            a_piece(1).wait_recv()
            b_piece(1, 1).start()
            b_piece(1, 3).start()
            side_start(1, 0)
            a_piece(3).wait_recv()
            a_piece(5).start()
            side_start(2, 0)

        for k in range(4):
            @pl.when(n == PART1[k])
            def _():
                if k == 3:
                    b_piece(3, 0).wait_recv()
                    b_piece(3, 4).start()
                b_piece(k, 3).wait_recv()
                b_piece(k, 5).start()
                if k < 2:
                    b_piece(k + 1, 0).wait_recv()
                    b_piece(k + 1, 4).start()
                b_piece(k, 1).wait_recv()
                side_start(k, 1)
                b_piece(k, 2).wait_recv()
                side_start(k, 2)
                if k == 0:
                    b_piece(2, 1).start()
                    b_piece(2, 3).start()
                if k == 1:
                    a_piece(4).wait_recv()
                    b_piece(3, 0).start()
                    b_piece(3, 2).start()
                    a_piece(5).wait_recv()
                    b_piece(3, 1).start()
                    b_piece(3, 3).start()
                    side_start(3, 0)

            @pl.when(n == PART2[k])
            def _():
                b_piece(k, 4).wait_recv()
                b_piece(k, 5).wait_recv()
                side_start(k, 3)

        @pl.when(n == 0)
        def _():
            m_core.wait_recv()
            for i in range(4):
                qsum[i] = part[c, i] + rcore[i]
            for m in m_z:
                m.start()

        @pl.when(n == 2)
        def _():
            for m in m_z:
                m.wait_recv()
            rz[3] = qsum[z] + rz[0] + rz[1] + rz[2]
            for m in m_y:
                m.start()

        @pl.when(n == 4)
        def _():
            for m in m_y:
                m.wait_recv()
            ry[3] = rz[3] + ry[0] + ry[1] + ry[2]
            m_x.start()

        @pl.when(n == 6)
        def _():
            m_x.wait_recv()
            small[2].wait()
            total = ry[3] + rx[...]
            inverse = lax.rsqrt(
                jnp.sum(total[:, 1152:1280], axis=1, keepdims=True) / D + 1e-05
            )
            cosine = ftab[:, 0:128]
            sine = ftab[:, 128:256]
            for j in range(8):
                head = total[:, j * 128 : (j + 1) * 128] * inverse
                qz[z, :, j * 128 : (j + 1) * 128] = rope(head, cosine, sine).astype(BF)
            qz[z, :, 1024:1152] = (total[:, 1024:1152] * inverse).astype(BF)
            for m in m_q:
                m.start()

        @pl.when(n == 8)
        def _():
            m_tab.wait_recv()
            small[3].wait()
            small[4].wait()
            m_bias.wait_recv()
            pbias[...] = pbias[...] + bias[0]
            cos_b = page[64:80, 0:HD]
            sin_b = page[64:80, HD : 2 * HD]
            sign = jnp.where(lane16 < HD // 2, -1.0, 1.0)
            for t in range(2):
                ref = ppage if t else page
                for p in range(48):
                    cos_a = ref[p : p + 1, 0:HD]
                    sin_a = ref[p : p + 1, HD : 2 * HD]
                    tabs[t, p * 16 : (p + 1) * 16, 0:HD] = cos_a * cos_b - sin_a * sin_b
                    tabs[t, p * 16 : (p + 1) * 16, HD : 2 * HD] = (
                        sin_a * cos_b + cos_a * sin_b
                    ) * sign

        @pl.when(n == 11)
        def _():
            for m in m_kv:
                m.wait_recv()
            small[5].wait()
            small[6].wait()
            for m in m_q:
                m.wait_recv()
            to_requests = (
                lane == (line % 32) // 4 * 16 + line // 32 * 4 + line % 4
            ).astype(F32).astype(BF)
            pad = jnp.zeros((112, 128), BF)
            for i in range(4):
                Bm[i] = jnp.zeros((128, 256), BF)
                Bm[i, 0:64, 0:128] = kub[i]
                Bm[i, 64:128, 128:256] = vub[i]
                heads = jnp.concatenate(
                    [qz[i, :, j * 128 : (j + 1) * 128] for j in range(8)], axis=0
                )
                Q[i] = jnp.dot(to_requests, heads, preferred_element_type=F32).astype(BF)
                fresh = jnp.dot(qz[i, :, 1024:1152], Bm[i], preferred_element_type=F32)
                FK[i] = jnp.concatenate(
                    [rope(fresh[:, 0:128], ftab[:, 0:128], ftab[:, 128:256]).astype(BF), pad],
                    axis=0,
                )
                FV[i] = jnp.concatenate([fresh[:, 128:256].astype(BF), pad], axis=0)

        for q, at in enumerate((0, 1, 2, 9)):
            @pl.when(n == at)
            def _():
                hlocal[q].wait()
                hremote[q].wait_recv()

        k = pick_int(n, lines)
        b = pick_int(n, places)

        @pl.when(n > 0)
        def _():
            side_piece(k, b, 0).wait_recv()
            side_piece(k, b, 1).wait_recv()

        yy, zz = place(offset_of(k), offset_of(b))

        def columns(xh, core):
            return pl.ds(pl.multiple_of((((yy * 2 + xh) * 2 + core) * 4 + zz) * 128, 128), 128)

        def tile(t, carry):
            left = jnp.concatenate(
                [H[t, :, columns(xh, core)] for xh in (0, 1) for core in (0, 1)], axis=1
            )
            right = jnp.concatenate([W[0, yy, zz], W[1, yy, zz]], axis=0)
            product = jnp.dot(left, right, preferred_element_type=F32)
            acc[t] += product
            return carry

        lax.fori_loop(0, 2, tile, 0)
        return carry

    lax.fori_loop(0, 16, step, 0)

    elsewhere = jnp.where((y + x + z) == 0, 0.0, masked_score)
    row32 = lax.broadcasted_iota(jnp.int32, (32, 128), 0)
    col32 = lax.broadcasted_iota(jnp.int32, (32, 128), 1)
    scaling = 1.0 / math.sqrt(HD)

    first_cz = ex[0]
    ex[0] += 3

    def partial_message(step):
        i = lax.rem(z + 1 + step, 4)
        return remote(
            ob.at[i], cz.at[step], es.at[first_cz + step], er.at[first_cz + step], dev(z_=i)
        )

    def group(step, carry):
        i = lax.rem(z + 1 + step, 4)
        lanes = pl.ds(pl.multiple_of(i * 128, 128), 128)
        for r in range(4):
            rows = slice(r * 192, (r + 1) * 192)
            at = slice(r * 32, (r + 1) * 32)
            seen = (col32 // 4 == r) & (col32 % 4 <= row32 % 4)
            mask = jnp.concatenate(
                [
                    jnp.broadcast_to(pbias[r : r + 1, :], (32, 384)),
                    jnp.where(seen, elsewhere, masked_score),
                ],
                axis=1,
            )
            latent = jnp.concatenate([acc[0, rows, lanes], acc[1, rows, lanes]], axis=0).astype(BF)
            rebuilt = jnp.dot(latent, Bm[i], preferred_element_type=F32)
            cosine = jnp.concatenate([tabs[0, rows, 0:128], tabs[1, rows, 0:128]], axis=0)
            sine = jnp.concatenate([tabs[0, rows, 128:256], tabs[1, rows, 128:256]], axis=0)
            keys = jnp.concatenate(
                [rope(rebuilt[:, 0:128], cosine, sine).astype(BF), FK[i]], axis=0
            )
            values = jnp.concatenate([rebuilt[:, 128:256].astype(BF), FV[i]], axis=0)
            scores = lax.dot_general(
                Q[i, at, :], keys, (((1,), (1,)), ((), ())), preferred_element_type=F32
            ) * scaling + mask
            peak = jnp.max(scores, axis=1, keepdims=True)
            e = jnp.where(mask > -1e29, jnp.exp(scores - peak), 0.0)
            total = jnp.sum(e, axis=1, keepdims=True)
            context = jnp.dot(e.astype(BF), values, preferred_element_type=F32)
            some = total > 0.0
            safe = jnp.where(some, total, 1.0)
            level = jnp.where(some, peak + jnp.log(safe), masked_score)
            ob[i, at, :] = (context / safe).astype(BF)
            lev[at, :] = jnp.broadcast_to(level, (32, HD))
        ob[i, 128:144, :] = coded(lev[:, 0:1])

        @pl.when(step < 3)
        def _():
            partial_message(step).start()

        return carry

    lax.fori_loop(0, 4, group, 0)

    m_cz = [partial_message(d) for d in range(3)]
    sent.extend(m_cz)
    for m in m_cz:
        m.wait_recv()
    value, level = merged([ob[z], cz[0], cz[1], cz[2]])
    cmine[0:128] = value.astype(BF)
    cmine[128:144] = coded(level)
    m_cy = [go(message(cmine, cy.at[d - 1], y_dev[d - 1])) for d in (1, 2, 3)]
    for m in m_cy:
        m.wait_recv()
    value, level = merged([cmine[...], cy[0], cy[1], cy[2]])
    cx[c, x, 0:128] = value.astype(BF)
    cx[c, x, 128:144] = coded(level)
    slot = cx.at[c, x]
    m_cx = [go(message(slot, slot, device)) for device in (xhi_dev, core_dev, dev(x_=1 - x, c_=o))]
    for m in m_cx:
        m.wait_recv()
    ocopy.wait()
    to_heads = (
        lane == (line % 16) // 4 * 32 + line // 16 * 4 + line % 4
    ).astype(F32).astype(BF)
    heads = []
    for g in range(2):
        value, _ = merged([cx[g, 0], cx[g, 1]])
        moved = jnp.dot(to_heads, value.astype(BF), preferred_element_type=F32).astype(BF)
        heads += [moved[j * 16 : (j + 1) * 16] for j in range(8)]
    fin[z] = jnp.dot(
        jnp.concatenate(heads, axis=1), OP[...], preferred_element_type=F32
    ).astype(BF)
    m_fin = [go(message(fin.at[z], fin.at[z], z_dev[d - 1])) for d in (1, 2, 3)]
    for m in m_fin:
        m.wait_recv()
    result = functools.reduce(jnp.add, [fin[d].astype(F32) for d in range(4)])
    for r in range(4):
        out_ref[r] = result[r * 4 : (r + 1) * 4].astype(BF)

    for copy in sent:
        copy.wait_send()
    for m in range(6):
        a_piece(m).wait_send()

    def drain(k, carry):
        for m in range(6):
            b_piece(k, m).wait_send()
        for b in range(4):
            @pl.when(k + b > 0)
            def _():
                side_piece(k, b, 0).wait_send()
                side_piece(k, b, 1).wait_send()
        return carry

    lax.fori_loop(0, 4, drain, 0)


MESSAGES = 1 + 6 + 3 + 3 + 3 + 1 + 3 + 3 + 3 + 3 + 3


def main(hid, down, picked, qproj, ku, vu, outp, page, bias, ftab):
    vm = pl.BlockSpec(memory_space=pltpu.VMEM)
    anyspace = pl.BlockSpec(memory_space=pl.ANY)
    V = pltpu.VMEM
    S = pltpu.SemaphoreType.DMA
    return pl.pallas_call(
        main_kernel,
        out_shape=jax.ShapeDtypeStruct((4, 4, 512), BF),
        in_specs=[anyspace] * 10,
        out_specs=vm,
        scratch_shapes=[
            V((128, 1024), BF),
            V((32, 128), BF),
            V((80, 256), F32),
            V((2, 8, 384), F32),
            V((16, 256), F32),
            V((2, 768, 8192), BF),
            V((2, 4, 4, 256, 512), BF),
            V((2, 768, 512), F32),
            V((128, 8192), BF),
            V((2048, 512), BF),
            V((4, 64, 128), BF),
            V((4, 64, 128), BF),
            V((2, 768, 256), F32),
            V((80, 256), F32),
            V((8, 384), F32),
            V((32, 128), BF),
            V((2, 4, 16, 1280), F32),
            V((4, 16, 1280), F32),
            V((4, 16, 1280), F32),
            V((4, 16, 1280), F32),
            V((4, 16, 1280), F32),
            V((16, 1280), F32),
            V((4, 16, 1152), BF),
            V((4, 128, 256), BF),
            V((4, 128, 128), BF),
            V((4, 128, 128), BF),
            V((4, 128, 128), BF),
            V((4, 144, 128), BF),
            V((128, 128), F32),
            V((3, 144, 128), BF),
            V((144, 128), BF),
            V((3, 144, 128), BF),
            V((2, 2, 144, 128), BF),
            V((4, 16, 512), BF),
            S((13,)),
            S((4,)),
            S((4,)),
            S((4,)),
            S((4,)),
            S((4,)),
            S((2,)),
            S((5, 6)),
            S((5, 6)),
            S((4, 4, 2)),
            S((4, 4, 2)),
            S((MESSAGES,)),
            S((MESSAGES,)),
        ],
        compiler_params=pltpu.CompilerParams(
            collective_id=0, has_side_effects=True, vmem_limit_bytes=62 * 2**20
        ),
        name="gather_decode",
    )(hid, down, picked, qproj, ku, vu, outp, page, bias, ftab)


def local(
    cached_hidden, page_order, lengths, new_ids, embedding,
    query_proj, down_proj, key_up, value_up, out_proj,
):
    requests, span, width = cached_hidden.shape
    frequency = 1.0 / rope_base ** (np.arange(HD // 2) * 2.0 / HD)
    freq = jnp.asarray(np.tile(np.concatenate([frequency, frequency]), (8, 1)).astype(np.float32))
    picked, page, fresh, bias = prepare(new_ids, page_order, lengths, freq, embedding)
    return main(
        cached_hidden.reshape(requests * span, width), down_proj, picked, query_proj, key_up,
        value_up, out_proj, page, bias, fresh,
    )


def solution(mesh):
    finer = Mesh(
        mesh.devices.reshape(mesh.shape["side"], 4, 2, 2, mesh.shape["head"]), AXES
    )
    placed = (
        P("side", SEQ_HEAD, None),
        P("side", SEQ_HEAD),
        P("side"),
        P(),
        P("side", SEQ_HEAD),
        P(SEQ_HEAD, None),
        P(SEQ_HEAD, None),
        P("head", None, None),
        P("head", None, None),
        P("head", SEQ),
    )
    return jax.shard_map(
        local, mesh=finer, in_specs=placed, out_specs=P("side", None, SEQ), check_vma=False
    )
```
